256 devices in a mesh: row: 16 (over y, z_lo), col: 16 (over z_hi, x, core).
Axes of the slice: x: 4, y: 4, z: 8 (z_hi: 2, z_lo: 4; z = z_hi * 4 + z_lo), core: 2. Of those that a mesh axis runs over, the one named last changes fastest.
Arguments:
- start_vectors: float32 [64, 32768], P(None, ('row', 'col')), may hold values from -6 to 6
- cluster_order: int32 [256, 128], P(('row', 'col')), may hold values from 0 to 127, each once within a row
- weights: bfloat16 [32768, 16, 2048], P('row', 'col'), may hold values from 0 to 1, as said below
- block_mask: int32 [256, 16, 16], P('row', 'col'), may hold values 0 or 1
Outputs:
- embedding: float32 [64, 32768], P(None, ('row', 'col'))
The draws below stay inside these ranges and needn't reach their ends.
Inputs may be any that keep to these rules, and one draw needn't show every extreme that they name: Each row of cluster_order holds every number of 0 to 127 once. `block_mask`: entries below the diagonal blocks are read only through their mirror. `weights`: every node except the last of its cluster block has a positive weight to the next node of its cluster block.
All inputs are finite; a program needn't handle non-finite values.
Results may differ from the reference program's by a relative error of at most 0.00087.
Values may be sent and summed in bfloat16 or wider, within the bound.
A program may use at most 64 MiB of HBM per device.

```python
import jax
import jax.numpy as jnp
from jax import lax

K = 64
NODE_DEV = 128
ITERS = 3
BLOCKS = 256
NODES = 32768
N_ROW = 16
N_COL = 16


def draw_weights(key, part):
    width = N_ROW * NODE_DEV
    near_share = min(1.0, 16.0 / NODE_DEV)
    far_share = min(1.0, 72.0 / (NODE_DEV * BLOCKS))
    entry = jnp.arange(width, dtype=jnp.int32)
    col_j = jnp.arange(N_COL, dtype=jnp.int32)
    col_nodes = ((entry // NODE_DEV)[None, :] * N_COL + col_j[:, None]) * NODE_DEV + (entry % NODE_DEV)[None, :]

    def one_block(block_id):
        block_key = jax.random.fold_in(key, block_id)
        keep_key, value_key = jax.random.split(block_key)
        row_nodes = block_id * NODE_DEV + jnp.arange(NODE_DEV, dtype=jnp.int32)
        same_block = (col_nodes // NODE_DEV)[None, :, :] == block_id
        chain_link = same_block & (col_nodes[None, :, :] == row_nodes[:, None, None] + 1)
        share = jnp.where(same_block, jnp.float32(near_share), jnp.float32(far_share))
        roll = jax.random.uniform(keep_key, (NODE_DEV, N_COL, width), jnp.float32)
        linked = (roll < share) | chain_link
        fresh = jax.random.uniform(value_key, (NODE_DEV, N_COL, width), jnp.float32)
        values = 0.05 + 0.95 * fresh
        return jnp.where(linked, values, jnp.float32(0.0)).astype(jnp.bfloat16)
    stacked = lax.map(one_block, jnp.arange(BLOCKS, dtype=jnp.int32))
    return stacked.reshape(NODES, N_COL, width)


def place_ends(entries, key, low, largest):
    longest = entries.shape.index(max(entries.shape))
    spots = []
    for shift in (0, 1):
        where = [jax.random.randint(jax.random.fold_in(key, axis), (), 0, length) for axis, length in enumerate(entries.shape)]
        where[longest] = (where[longest] + shift) % entries.shape[longest]
        spots.append(tuple(where))
    return entries.at[spots[0]].set(low).at[spots[1]].set(largest)


def block_levels(rng, shape, cuts, low, largest):
    factor_of, own = 1.0, jax.random.fold_in(rng, 6)
    for axis_at, blocks in cuts:
        steps = jnp.exp(jax.random.uniform(jax.random.fold_in(own, axis_at), (blocks,), jnp.float32, low / len(cuts), largest / len(cuts)))
        factor_of = factor_of * jnp.repeat(steps, shape[axis_at] // blocks).reshape([-1 if axis == axis_at else 1 for axis in range(len(shape))])
    return factor_of


def gaussian(own_key, dims, spread, reach, cuts=(), kind=jnp.bfloat16):
    level = block_levels(own_key, dims, cuts, -0.22, 0.18) if cuts else 1.0
    drawn = jax.random.normal(own_key, dims, jnp.float32) * spread * level
    return jnp.minimum(jnp.maximum(drawn, -reach), reach).astype(kind)


def setup_inputs(seed: int = 0) -> dict:
    keys = jax.random.split(jax.random.key(seed), 5)
    return {
        "start_vectors": gaussian(keys[0], (K, NODES), 1.0, 6.0, ((1, 256),), jnp.float32),
        "cluster_order": jax.vmap(lambda own: jax.random.permutation(own, NODE_DEV))(jax.random.split(keys[1], BLOCKS)).reshape((BLOCKS, NODE_DEV)).astype(jnp.int32),
        "weights": draw_weights(jax.random.fold_in(keys[4], 71), 0),
        "block_mask": place_ends((jax.random.randint(keys[3], (BLOCKS, N_COL, N_ROW), 0, 3) < 1).astype(jnp.int32), jax.random.fold_in(keys[3], 1), 0, 1),
    }


def orthonormalize(panel_in):
    gram_matrix = jnp.dot(panel_in.astype(jnp.float32), panel_in.T.astype(jnp.float32), precision=lax.Precision.HIGHEST, preferred_element_type=jnp.float32)
    factor = jnp.linalg.cholesky(gram_matrix)
    return jax.scipy.linalg.solve_triangular(factor, panel_in, lower=True)

def block_row(weights, block_mask, block_id):
    stored = lax.dynamic_slice_in_dim(weights, block_id * NODE_DEV, NODE_DEV, 0)
    stored = stored.reshape(NODE_DEV, N_COL, N_ROW, NODE_DEV).transpose(0, 2, 1, 3).reshape(NODE_DEV, NODES)
    mask_row = lax.dynamic_index_in_dim(block_mask, block_id, 0, keepdims=False).T.reshape(BLOCKS)
    span_ids = jnp.arange(BLOCKS, dtype=jnp.int32)
    live_cols = jnp.repeat((mask_row > 0) | (span_ids == block_id), NODE_DEV)
    row_nodes = block_id * NODE_DEV + jnp.arange(NODE_DEV, dtype=jnp.int32)
    col_nodes = jnp.arange(NODES, dtype=jnp.int32)
    keep_upper = live_cols[None, :] & (row_nodes[:, None] < col_nodes[None, :])
    return jnp.where(keep_upper, stored, jnp.zeros((), stored.dtype))

def apply_graph(weights, block_mask, vectors):

    def visit(carry, block_id):
        upper_rows = block_row(weights, block_mask, block_id)
        direct = jnp.dot(vectors.astype(jnp.float32), upper_rows.T.astype(jnp.float32), preferred_element_type=jnp.float32)
        local_vec = lax.dynamic_slice_in_dim(vectors, block_id * NODE_DEV, NODE_DEV, 1)
        carry = carry + jnp.dot(local_vec.astype(jnp.float32), upper_rows.astype(jnp.float32), preferred_element_type=jnp.float32)
        return (carry, direct)
    initial_sum = jnp.zeros((vectors.shape[0], NODES), jnp.float32)
    mirrored, direct_rows = lax.scan(visit, initial_sum, jnp.arange(BLOCKS, dtype=jnp.int32))
    direct_all = direct_rows.transpose(1, 0, 2).reshape(vectors.shape[0], NODES)
    return direct_all + mirrored

def reference(start_vectors, cluster_order, weights, block_mask):
    ones_row = jnp.ones((1, NODES), weights.dtype)
    degree = apply_graph(weights, block_mask, ones_row)
    inverse_root = 1.0 / jnp.sqrt(degree)
    reshaped = start_vectors.reshape(K, BLOCKS, NODE_DEV)
    picked = jnp.take_along_axis(reshaped, jnp.broadcast_to(cluster_order[None], reshaped.shape), axis=2)
    panel_now = orthonormalize(picked.reshape(K, NODES))
    for round_index in range(ITERS):
        vectors = (inverse_root * panel_now).astype(jnp.bfloat16)
        product = apply_graph(weights, block_mask, vectors)
        panel_now = orthonormalize(panel_now + inverse_root * product)
    return jnp.sqrt(jnp.float32(NODES)) * panel_now
```

```python
import functools
import math

import jax
import jax.numpy as jnp
from jax import lax
from jax.experimental import pallas as pl
from jax.experimental.pallas import tpu as pltpu
from jax.sharding import PartitionSpec as P

ITERS = 3
K = 64
B = 128
NY, NL, NH, NX, NC = 4, 4, 2, 4, 2
MESH = pl.DeviceIdType.MESH
HI = lax.Precision.HIGHEST
F32 = jnp.float32
BF = jnp.bfloat16


def inverse_factor(packed):
    half = K // 2
    low = lax.broadcasted_iota(jnp.int32, (half, 2 * K), 1) < K
    row_id = lax.broadcasted_iota(jnp.int32, (half, 2 * K), 0)
    lane_id = lax.broadcasted_iota(jnp.int32, (half, 2 * K), 1)
    top = jnp.where(low, (row_id == lane_id).astype(F32), pltpu.roll(packed, K, 1))
    bottom = jnp.where(low, (row_id + half == lane_id).astype(F32), packed)
    rows = [top[8 * g : 8 * g + 8] for g in range(half // 8)]
    rows += [bottom[8 * g : 8 * g + 8] for g in range(half // 8)]
    sub = lax.broadcasted_iota(jnp.int32, (8, 2 * K), 0)
    groups = K // 8
    for j in range(K):
        first, s = divmod(j, 8)
        pivot_row = jnp.broadcast_to(rows[first][s : s + 1, :], (8, 2 * K))
        pivot = jnp.broadcast_to(pivot_row[:, K + j : K + j + 1], (8, 2 * K))
        scaled = pivot_row / pivot
        for g in range(first, groups):
            column = jnp.broadcast_to(rows[g][:, K + j : K + j + 1], (8, 2 * K))
            if g == first:
                if s == 7:
                    continue
                column = jnp.where(sub > s, column, 0.0)
            rows[g] = rows[g] - column * scaled
    out = []
    for g in range(groups):
        lane = lax.broadcasted_iota(jnp.int32, (8, 2 * K), 1)
        on_diag = lane == sub + (K + 8 * g)
        diag = jnp.sum(jnp.where(on_diag, rows[g], 0.0), axis=1, keepdims=True)
        out.append(rows[g] * (1.0 / jnp.sqrt(diag)))
    return jnp.concatenate(out, axis=0)[:, :K]


def kernel(
    start_ref,
    order_ref,
    mask_ref,
    w_ref,
    out_ref,
    matrix,
    wdiag,
    vsend,
    vrow,
    vcol,
    dsum,
    d1,
    d2,
    rc,
    rx,
    rz,
    msum,
    m1,
    ry,
    rl,
    edsum,
    ed1,
    ed2,
    erc,
    erx,
    erz,
    emsum,
    em1,
    ery,
    erl,
    gs,
    ga,
    gb,
    gy,
    gl,
    wsem,
    ssem,
    rsem,
):
    r = lax.axis_index("row")
    c = lax.axis_index("col")
    y, l = r // NL, r % NL
    h, e = c // (NX * NC), c % (NX * NC)
    x, core = e // NC, e % NC

    chunk_copies = []
    for a in range(16):
        cp = pltpu.make_async_copy(
            w_ref.at[pl.ds(a * B, B), :], matrix.at[pl.ds(a * B, B), :], wsem.at[a]
        )
        cp.start()
        chunk_copies.append(cp)
    diag_copy = pltpu.make_async_copy(
        w_ref.at[pl.ds(pl.multiple_of(c * B, B), B), pl.ds(pl.multiple_of(r * B, B), B)],
        wdiag,
        wsem.at[16],
    )
    diag_copy.start()

    barrier = pltpu.get_barrier_semaphore()
    for d in range(1, 16):
        pl.semaphore_signal(
            barrier, inc=1, device_id=(r, (c + d) % 16), device_id_type=MESH
        )
        pl.semaphore_signal(
            barrier, inc=1, device_id=((r + d) % 16, c), device_id_type=MESH
        )

    count = [0]
    pending = []

    def slot():
        count[0] += 1
        return count[0] - 1

    def send(src, dst, row, col, index):
        cp = pltpu.make_async_remote_copy(
            src_ref=src,
            dst_ref=dst,
            send_sem=ssem.at[index],
            recv_sem=rsem.at[index],
            device_id=(row, col),
            device_id_type=MESH,
        )
        cp.start()
        pending.append(cp)
        return cp

    def col_of(hh, ee):
        return hh * (NX * NC) + ee

    def row_of(yy, ll):
        return yy * NL + ll

    def gram_start(t, panel):
        gram = lax.dot_general(
            panel, panel, (((1,), (1,)), ((), ())), precision=HI, preferred_element_type=F32
        )
        gs[t, 0] = jnp.concatenate([gram[: K // 2], gram[K // 2 :]], axis=1)
        cps = []
        for d in range(1, NX * NC):
            cps.append(send(gs.at[t, 0], ga.at[t, d - 1], r, col_of(h, (e + d) % 8), slot()))
        return cps

    def gram_h(t, cps):
        for cp in cps:
            cp.wait_recv()
        total = gs[t, 0]
        for d in range(7):
            total = total + ga[t, d]
        gs[t, 1] = total
        return [send(gs.at[t, 1], gb.at[t], r, col_of(1 - h, e), slot())]

    def gram_y(t, cps):
        for cp in cps:
            cp.wait_recv()
        gs[t, 2] = gs[t, 1] + gb[t]
        out = []
        for d in range(1, NY):
            out.append(send(gs.at[t, 2], gy.at[t, d - 1], row_of((y + d) % NY, l), c, slot()))
        return out

    def gram_l(t, cps):
        for cp in cps:
            cp.wait_recv()
        gs[t, 3] = ((gs[t, 2] + gy[t, 0]) + gy[t, 1]) + gy[t, 2]
        out = []
        for d in range(1, NL):
            out.append(send(gs.at[t, 3], gl.at[t, d - 1], row_of(y, (l + d) % NL), c, slot()))
        return out

    def gram_end(t, cps):
        for cp in cps:
            cp.wait_recv()
        return inverse_factor(((gs[t, 3] + gl[t, 0]) + gl[t, 1]) + gl[t, 2])

    def rs_core(src, dst):
        return [send(src.at[1 - core], dst, r, col_of(h, x * NC + 1 - core), slot())]

    def rs_x(cps, src, got, mid, dst):
        for cp in cps:
            cp.wait_recv()
        mid[...] = src[core] + got[...]
        out = []
        for d in range(1, NX):
            xx = (x + d) % NX
            out.append(send(mid.at[xx], dst.at[d - 1], r, col_of(h, xx * NC + core), slot()))
        return out

    def rs_h(cps, mid, got, last, dst):
        for cp in cps:
            cp.wait_recv()
        last[...] = ((mid[x] + got[0]) + got[1]) + got[2]
        return [send(last.at[1 - h], dst, r, col_of(1 - h, e), slot())]

    def rs_y(src, dst):
        out = []
        for d in range(1, NY):
            yy = (y + d) % NY
            out.append(send(src.at[yy], dst.at[d - 1], row_of(yy, l), c, slot()))
        return out

    def rs_l(cps, src, got, mid, dst):
        for cp in cps:
            cp.wait_recv()
        mid[...] = ((src[y] + got[0]) + got[1]) + got[2]
        out = []
        for d in range(1, NL):
            ll = (l + d) % NL
            out.append(send(mid.at[ll], dst.at[d - 1], row_of(y, ll), c, slot()))
        return out

    def wait_all(cps):
        for cp in cps:
            cp.wait_recv()

    order = order_ref[...]
    pick = (lax.broadcasted_iota(jnp.int32, (B, B), 0) == jnp.broadcast_to(order, (B, B))).astype(F32)
    panel = jnp.dot(start_ref[...], pick, precision=HI, preferred_element_type=F32)
    pl.semaphore_wait(barrier, 30)
    gram_cps = gram_start(0, panel)

    spread = (
        lax.broadcasted_iota(jnp.int32, (16, 16 * B), 1) // B
        == lax.broadcasted_iota(jnp.int32, (16, 16 * B), 0)
    ).astype(F32)
    live = jnp.dot((mask_ref[...] > 0).astype(F32), spread, preferred_element_type=F32)
    col_block = lax.broadcasted_iota(jnp.int32, (1, 16 * B), 1) // B * 16 + c
    ones_wide = jnp.ones((8, 16 * B), BF)
    ones_rows = jnp.ones((8, B), BF)
    diag_copy.wait()
    upper = lax.broadcasted_iota(jnp.int32, (B, B), 0) < lax.broadcasted_iota(jnp.int32, (B, B), 1)
    diag_value = jnp.where(upper, wdiag[...].astype(F32), 0.0).astype(BF)
    col_totals = jnp.zeros((8, 16 * B), F32)
    for a in range(16):
        chunk_copies[a].wait()
        keep = jnp.where((live[a : a + 1, :] > 0.5) & (col_block > r * 16 + a), 1.0, 0.0).astype(BF)
        rows = pl.ds(a * B, B)
        matrix[rows, :] = matrix[rows, :] * jnp.broadcast_to(keep, (B, 16 * B))
    matrix[pl.ds(pl.multiple_of(c * B, B), B), pl.ds(pl.multiple_of(r * B, B), B)] = diag_value
    gram_cps = gram_h(0, gram_cps)
    for a in range(16):
        rows = pl.ds(a * B, B)
        block = matrix[rows, :]
        col_totals = col_totals + jnp.dot(ones_rows, block, preferred_element_type=F32)
        edsum[a % 2, a // 2 % 4, a // 8] = lax.dot_general(
            ones_wide, block, (((1,), (1,)), ((), ())), preferred_element_type=F32
        )
    for i in range(16):
        emsum[i // NL, i % NL] = col_totals[:, i * B : (i + 1) * B]
    cps_c = rs_core(edsum, erc)
    cps_r = rs_y(emsum, ery)
    cps_c = rs_x(cps_c, edsum, erc, ed1, erx)
    cps_r = rs_l(cps_r, emsum, ery, em1, erl)
    gram_cps = gram_y(0, gram_cps)
    cps_c = rs_h(cps_c, ed1, erx, ed2, erz)
    gram_cps = gram_l(0, gram_cps)
    wait_all(cps_r)
    wait_all(cps_c)
    degree = (ed2[h] + erz[...]) + (((em1[l] + erl[0]) + erl[1]) + erl[2])
    inverse_root = jnp.broadcast_to(1.0 / jnp.sqrt(degree[0:1, :]), (K, B))
    factor = gram_end(0, gram_cps)
    panel = jnp.dot(factor, panel, precision=HI, preferred_element_type=F32)

    for t in range(ITERS):
        vectors = (inverse_root * panel).astype(BF)
        vsend[t] = vectors
        vrow[t, c] = vectors
        vcol[t, r] = vectors
        own = vsend.at[t]
        cps_h = send(own, vrow.at[t, c], r, col_of(1 - h, e), slot())
        cps_l = []
        for d in range(1, NL):
            cps_l.append(send(own, vcol.at[t, r], row_of(y, (l + d) % NL), c, slot()))
        cps_e = []
        for d in range(1, 8):
            cps_e.append(send(own, vrow.at[t, c], r, col_of(h, (e + d) % 8), slot()))
        cps_y = []
        for d in range(1, NY):
            cps_y.append(send(own, vcol.at[t, r], row_of((y + d) % NY, l), c, slot()))
        if t > 0:
            gram_cps = gram_start(t, panel)
        for d in range(1, NL):
            cps_l[d - 1].wait_recv()
            from_l = row_of(y, (l - d + NL) % NL)
            for f in range(1, NY):
                cps_y.append(
                    send(vcol.at[t, from_l], vcol.at[t, from_l], row_of((y + f) % NY, l), c, slot())
                )
        cps_h.wait_recv()
        other = col_of(1 - h, e)
        for d in range(1, 8):
            cps_e.append(send(vrow.at[t, other], vrow.at[t, other], r, col_of(h, (e + d) % 8), slot()))
        if t > 0:
            gram_cps = gram_h(t, gram_cps)
        wait_all(cps_e)
        wide = jnp.concatenate([vrow[t, i] for i in range(16)], axis=1)

        def mirror_step(j, _):
            out = jnp.dot(
                wide,
                matrix[:, pl.ds(pl.multiple_of(j * 2 * B, 2 * B), 2 * B)],
                preferred_element_type=F32,
            )
            msum[t, j // 2, 2 * (j % 2)] = out[:, :B]
            msum[t, j // 2, 2 * (j % 2) + 1] = out[:, B:]
            return 0

        lax.fori_loop(0, 8, mirror_step, 0)
        cps_r = rs_y(msum.at[t], ry.at[t])
        if t > 0:
            gram_cps = gram_y(t, gram_cps)
        wait_all(cps_y)
        wide_c = jnp.concatenate([vcol[t, i] for i in range(16)], axis=1)

        def direct_step(j, _):
            out = lax.dot_general(
                wide_c,
                matrix[pl.ds(pl.multiple_of(j * 2 * B, 2 * B), 2 * B), :],
                (((1,), (1,)), ((), ())),
                preferred_element_type=F32,
            )
            dsum[t, 0, j % 4, j // 4] = out[:, :B]
            dsum[t, 1, j % 4, j // 4] = out[:, B:]
            return 0

        lax.fori_loop(0, 8, direct_step, 0)
        cps_c = rs_core(dsum.at[t], rc.at[t])
        if t > 0:
            gram_cps = gram_l(t, gram_cps)
        cps_c = rs_x(cps_c, dsum.at[t], rc.at[t], d1.at[t], rx.at[t])
        cps_r = rs_l(cps_r, msum.at[t], ry.at[t], m1.at[t], rl.at[t])
        cps_c = rs_h(cps_c, d1.at[t], rx.at[t], d2.at[t], rz.at[t])
        if t > 0:
            factor = gram_end(t, gram_cps)
        wait_all(cps_r)
        wait_all(cps_c)
        product = (d2[t, h] + rz[t]) + (((m1[t, l] + rl[t, 0]) + rl[t, 1]) + rl[t, 2])
        panel = panel + inverse_root * product
        if t > 0:
            panel = jnp.dot(factor, panel, precision=HI, preferred_element_type=F32)

    gram_cps = gram_start(ITERS, panel)
    gram_cps = gram_h(ITERS, gram_cps)
    gram_cps = gram_y(ITERS, gram_cps)
    gram_cps = gram_l(ITERS, gram_cps)
    factor = gram_end(ITERS, gram_cps)
    out_ref[...] = jnp.dot(factor, panel, precision=HI, preferred_element_type=F32)
    for cp in pending:
        cp.wait_send()


def copies():
    gram = 7 + 1 + 3 + 3
    scatter = 1 + 3 + 1 + 3 + 3
    gather = 1 + 3 + 7 + 3 + 9 + 7
    return (ITERS + 1) * (gram + scatter) + ITERS * gather


def local(start_vectors, cluster_order, weights, block_mask):
    vm = pltpu.VMEM
    n = ITERS
    blk = (K, B)
    eblk = (8, B)
    g = (K // 2, 2 * K)
    scratch = [
        vm((16 * B, 16 * B), BF),
        vm((B, B), BF),
        vm((n,) + blk, BF),
        vm((n, 16) + blk, BF),
        vm((n, 16) + blk, BF),
        vm((n, NC, NX, NH) + blk, F32),
        vm((n, NX, NH) + blk, F32),
        vm((n, NH) + blk, F32),
        vm((n, NX, NH) + blk, F32),
        vm((n, NX - 1, NH) + blk, F32),
        vm((n,) + blk, F32),
        vm((n, NY, NL) + blk, F32),
        vm((n, NL) + blk, F32),
        vm((n, NY - 1, NL) + blk, F32),
        vm((n, NL - 1) + blk, F32),
        vm((NC, NX, NH) + eblk, F32),
        vm((NX, NH) + eblk, F32),
        vm((NH,) + eblk, F32),
        vm((NX, NH) + eblk, F32),
        vm((NX - 1, NH) + eblk, F32),
        vm(eblk, F32),
        vm((NY, NL) + eblk, F32),
        vm((NL,) + eblk, F32),
        vm((NY - 1, NL) + eblk, F32),
        vm((NL - 1,) + eblk, F32),
        vm((n + 1, 4) + g, F32),
        vm((n + 1, 7) + g, F32),
        vm((n + 1,) + g, F32),
        vm((n + 1, 3) + g, F32),
        vm((n + 1, 3) + g, F32),
        pltpu.SemaphoreType.DMA((17,)),
        pltpu.SemaphoreType.DMA((copies(),)),
        pltpu.SemaphoreType.DMA((copies(),)),
    ]
    space = pl.BlockSpec(memory_space=pltpu.VMEM)
    panel = pl.pallas_call(
        kernel,
        out_shape=jax.ShapeDtypeStruct(blk, F32),
        in_specs=[space, space, space, pl.BlockSpec(memory_space=pltpu.HBM)],
        out_specs=space,
        scratch_shapes=scratch,
        compiler_params=pltpu.CompilerParams(
            collective_id=0, has_side_effects=True, vmem_limit_bytes=48 * 1024 * 1024
        ),
    )(start_vectors, cluster_order, block_mask[:, 0, :], weights[:, 0, :])
    return math.sqrt(16 * 16 * B) * panel


def solution(mesh):
    placed = (
        P(None, ("row", "col")),
        P(("row", "col"), None),
        P("row", "col", None),
        P("row", "col", None),
    )
    return jax.shard_map(
        local, mesh=mesh, in_specs=placed, out_specs=P(None, ("row", "col")), check_vma=False
    )
```

```python
import functools
import math

import jax
import jax.numpy as jnp
from jax import lax
from jax.experimental import pallas as pl
from jax.experimental.pallas import tpu as pltpu
from jax.sharding import PartitionSpec as P

ITERS = 3
K = 64
B = 128
NY, NL, NH, NX, NC = 4, 4, 2, 4, 2
MESH = pl.DeviceIdType.MESH
HI = lax.Precision.HIGHEST
F32 = jnp.float32
BF = jnp.bfloat16


def inverse_factor(blocks):
    groups = K // 8
    lane = lax.broadcasted_iota(jnp.int32, (8, 2 * K), 1)
    sub = lax.broadcasted_iota(jnp.int32, (8, 2 * K), 0)
    rows = [
        jnp.where(lane < K, (lane == sub + 8 * g).astype(F32), blocks[g]) for g in range(groups)
    ]

    def row_of_all(value, k):
        return jnp.broadcast_to(value[k : k + 1, :], (8, 2 * K))

    def column_of_all(value, j):
        return jnp.broadcast_to(value[:, K + j : K + j + 1], (8, 2 * K))

    out = []
    for b in range(groups):
        block = rows[b]
        columns = [column_of_all(block, 8 * b + m) for m in range(8)]
        pivots = {(k, m): row_of_all(columns[m], k) for m in range(8) for k in range(m, 8)}
        lower, inverses, reduced = {}, [], []
        for m in range(8):
            inverses.append(1.0 / pivots[m, m])
            for k in range(m + 1, 8):
                lower[k, m] = pivots[k, m] * inverses[m]
            for k in range(m + 1, 8):
                for n in range(m + 1, k + 1):
                    pivots[k, n] = pivots[k, n] - lower[k, m] * pivots[n, m]
        for k in range(8):
            value = row_of_all(block, k)
            for m in range(k):
                value = value - lower[k, m] * reduced[m]
            reduced.append(value)
        if b + 1 < groups:
            solved = [None] * 8
            for k in reversed(range(8)):
                value = reduced[k] * inverses[k]
                for n in range(k + 1, 8):
                    value = value - lower[n, k] * solved[n]
                solved[k] = value
            for g in range(b + 1, groups):
                value = rows[g]
                for k in range(8):
                    value = value - column_of_all(rows[g], 8 * b + k) * solved[k]
                rows[g] = value
        result = jnp.zeros((8, 2 * K), F32)
        for k in range(8):
            result = jnp.where(sub == k, reduced[k] * (1.0 / jnp.sqrt(pivots[k, k])), result)
        out.append(result)
    return jnp.concatenate(out, axis=0)[:, :K]


def kernel(
    start_hbm,
    order_hbm,
    mask_hbm,
    w_ref,
    out_ref,
    start_ref,
    order_ref,
    mask_ref,
    matrix,
    wdiag,
    vsend,
    vrow,
    vcol,
    dsum,
    d1,
    d2,
    rc,
    xq,
    xm,
    rz,
    msum,
    m1,
    yq,
    ym,
    rl,
    edsum,
    ed1,
    ed2,
    erc,
    erx,
    erz,
    emsum,
    em1,
    ery,
    erl,
    gs,
    ga,
    g1,
    gy,
    g2,
    gz,
    gf,
    wsem,
    ssem,
    rsem,
):
    r = lax.axis_index("row")
    c = lax.axis_index("col")
    y, l = r // NL, r % NL
    h, e = c // (NX * NC), c % (NX * NC)
    x, core = e // NC, e % NC
    z = h * NL + l
    rest = NX * NC

    def col_of(hh, ee):
        return hh * rest + ee

    def row_of(yy, ll):
        return yy * NL + ll

    barrier = pltpu.get_barrier_semaphore()
    for d in range(1, NH * NL):
        zz = (z + d) % (NH * NL)
        pl.semaphore_signal(
            barrier,
            inc=1,
            device_id=(row_of(y, zz % NL), col_of(zz // NL, e)),
            device_id_type=MESH,
        )
    for d in range(1, NY):
        pl.semaphore_signal(
            barrier, inc=1, device_id=(row_of((y + d) % NY, l), c), device_id_type=MESH
        )
    for d in range(1, rest):
        pl.semaphore_signal(
            barrier, inc=1, device_id=(r, col_of(h, (e + d) % rest)), device_id_type=MESH
        )

    local_copies = []
    for i, (src, dst) in enumerate(
        ((order_hbm, order_ref), (start_hbm, start_ref), (mask_hbm, mask_ref))
    ):
        cp = pltpu.make_async_copy(src, dst, wsem.at[17 + i])
        cp.start()
        local_copies.append(cp)
    chunk_copies = []
    for a in range(16):
        cp = pltpu.make_async_copy(
            w_ref.at[pl.ds(a * B, B), :], matrix.at[pl.ds(a * B, B), :], wsem.at[a]
        )
        cp.start()
        chunk_copies.append(cp)
    diag_copy = pltpu.make_async_copy(
        w_ref.at[pl.ds(pl.multiple_of(c * B, B), B), pl.ds(pl.multiple_of(r * B, B), B)],
        wdiag,
        wsem.at[16],
    )
    diag_copy.start()

    count = [0]
    pending = []

    def send(src, dst, row, col):
        index = count[0]
        count[0] += 1
        cp = pltpu.make_async_remote_copy(
            src_ref=src,
            dst_ref=dst,
            send_sem=ssem.at[index],
            recv_sem=rsem.at[index],
            device_id=(row, col),
            device_id_type=MESH,
        )
        cp.start()
        pending.append(cp)
        return cp

    def wait_all(cps):
        for cp in cps:
            cp.wait_recv()

    def gram_local(t, panel):
        padded = jnp.concatenate([jnp.zeros((K, B), F32), panel], axis=0)
        gram = lax.dot_general(
            panel, padded, (((1,), (1,)), ((), ())), precision=HI, preferred_element_type=F32
        )
        for g in range(8):
            gs[t, g] = gram[8 * g : 8 * g + 8]

    def gram_start(t):
        return [
            send(gs.at[t, (e + d) % rest], ga.at[t, d - 1], r, col_of(h, (e + d) % rest))
            for d in range(1, rest)
        ]

    def gram_y(t, cps):
        wait_all(cps)
        total = gs[t, e]
        for d in range(rest - 1):
            total = total + ga[t, d]
        g1[t] = total
        return [
            send(g1.at[t], gy.at[t, d - 1], row_of((y + d) % NY, l), c) for d in range(1, NY)
        ]

    def gram_z(t, cps):
        wait_all(cps)
        g2[t] = ((g1[t] + gy[t, 0]) + gy[t, 1]) + gy[t, 2]
        out = []
        for d in range(1, NH * NL):
            zz = (z + d) % (NH * NL)
            out.append(send(g2.at[t], gz.at[t, d - 1], row_of(y, zz % NL), col_of(zz // NL, e)))
        return out

    def gram_all(t, cps):
        wait_all(cps)
        total = g2[t]
        for d in range(NH * NL - 1):
            total = total + gz[t, d]
        gf[t, e] = total
        return [
            send(gf.at[t, e], gf.at[t, e], r, col_of(h, (e + d) % rest)) for d in range(1, rest)
        ]

    def gram_end(t, cps):
        wait_all(cps)
        return inverse_factor([gf[t, g] for g in range(8)])

    def rs_core(src, dst):
        return [send(src.at[1 - core], dst, r, col_of(h, x * NC + 1 - core))]

    def rs_h(last, dst):
        return [send(last.at[1 - h], dst, r, col_of(1 - h, e))]

    def rs_l(mid, dst):
        out = []
        for d in range(1, NL):
            ll = (l + d) % NL
            out.append(send(mid.at[ll], dst.at[d - 1], row_of(y, ll), c))
        return out

    first, second = pl.ds(0, K // 2), pl.ds(K // 2, K // 2)

    def ring_start(src, q, p, device):
        ahead, behind, across = (p + 1) % 4, (p + 3) % 4, (p + 2) % 4
        return [
            send(src.at[across, :, first, :], q.at[0], *device(ahead)),
            send(src.at[across, :, second, :], q.at[1], *device(behind)),
            send(src.at[ahead, :, second, :], q.at[2], *device(ahead)),
            send(src.at[behind, :, first, :], q.at[3], *device(behind)),
        ]

    def ring_mid(cps, src, q, mid, p, device):
        ahead, behind = (p + 1) % 4, (p + 3) % 4
        cps[0].wait_recv()
        mid[0] = src[ahead, :, first, :] + q[0]
        forth = send(mid.at[0], q.at[4], *device(ahead))
        cps[1].wait_recv()
        mid[1] = src[behind, :, second, :] + q[1]
        back = send(mid.at[1], q.at[5], *device(behind))
        return cps[2:] + [forth, back]

    def ring_end(cps, src, q, p, dst):
        wait_all(cps)
        dst[:, first, :] = (src[p, :, first, :] + q[3]) + q[4]
        dst[:, second, :] = (src[p, :, second, :] + q[2]) + q[5]

    def device_x(p):
        return r, col_of(h, p * NC + core)

    def device_y(p):
        return row_of(p, l), c

    local_copies[0].wait()
    local_copies[1].wait()
    pick = (
        lax.broadcasted_iota(jnp.int32, (B, B), 0) == jnp.broadcast_to(order_ref[...], (B, B))
    ).astype(F32)
    panel = jnp.dot(start_ref[...], pick, precision=HI, preferred_element_type=F32)
    gram_local(0, panel)

    local_copies[2].wait()
    mask = jnp.concatenate([mask_ref[a] for a in range(16)], axis=0)
    spread = (
        lax.broadcasted_iota(jnp.int32, (16, 16 * B), 1) // B
        == lax.broadcasted_iota(jnp.int32, (16, 16 * B), 0)
    ).astype(F32)
    live = jnp.dot((mask > 0).astype(F32), spread, preferred_element_type=F32)
    col_block = lax.broadcasted_iota(jnp.int32, (1, 16 * B), 1) // B * 16 + c
    ones_wide = jnp.ones((8, 16 * B), BF)
    ones_rows = jnp.ones((8, B), BF)
    col_totals = jnp.zeros((8, 16 * B), F32)
    for a in range(16):
        chunk_copies[a].wait()
        keep = jnp.where((live[a : a + 1, :] > 0.5) & (col_block > r * 16 + a), 1.0, 0.0)
        rows = pl.ds(a * B, B)
        block = matrix[rows, :] * jnp.broadcast_to(keep.astype(BF), (B, 16 * B))
        matrix[rows, :] = block
        col_totals = col_totals + jnp.dot(ones_rows, block, preferred_element_type=F32)
        edsum[a % 2, a // 2 % 4, a // 8] = lax.dot_general(
            ones_wide, block, (((1,), (1,)), ((), ())), preferred_element_type=F32
        )
    for i in range(16):
        emsum[i // NL, i % NL] = col_totals[:, i * B : (i + 1) * B]
    diag_copy.wait()
    upper = lax.broadcasted_iota(jnp.int32, (B, B), 0) < lax.broadcasted_iota(jnp.int32, (B, B), 1)
    diag_value = jnp.where(upper, wdiag[...].astype(F32), 0.0).astype(BF)
    matrix[pl.ds(pl.multiple_of(c * B, B), B), pl.ds(pl.multiple_of(r * B, B), B)] = diag_value
    diag_degree = jnp.dot(ones_rows, diag_value, preferred_element_type=F32) + lax.dot_general(
        ones_rows, diag_value, (((1,), (1,)), ((), ())), preferred_element_type=F32
    )

    pl.semaphore_wait(barrier, NH * NL - 1 + NY - 1 + rest - 1)
    gram_cps = gram_start(0)
    cps_c = rs_core(edsum, erc)
    cps_r = [
        send(emsum.at[(y + d) % NY], ery.at[d - 1], row_of((y + d) % NY, l), c)
        for d in range(1, NY)
    ]
    wait_all(cps_c)
    ed1[...] = edsum[core] + erc[...]
    cps_c = [
        send(ed1.at[(x + d) % NX], erx.at[d - 1], *device_x((x + d) % NX)) for d in range(1, NX)
    ]
    gram_cps = gram_y(0, gram_cps)
    wait_all(cps_r)
    em1[...] = ((emsum[y] + ery[0]) + ery[1]) + ery[2]
    cps_r = rs_l(em1, erl)
    wait_all(cps_c)
    ed2[...] = ((ed1[x] + erx[0]) + erx[1]) + erx[2]
    cps_c = rs_h(ed2, erz)
    gram_cps = gram_z(0, gram_cps)
    wait_all(cps_r)
    wait_all(cps_c)
    degree = (ed2[h] + erz[...]) + (((em1[l] + erl[0]) + erl[1]) + erl[2]) + diag_degree
    inverse_root = jnp.broadcast_to(1.0 / jnp.sqrt(degree[0:1, :]), (K, B))
    gram_cps = gram_all(0, gram_cps)
    factor = gram_end(0, gram_cps)
    panel = jnp.dot(factor, panel, precision=HI, preferred_element_type=F32)

    half = 8 * B
    quarter = 4 * B
    pair = 2 * B

    for t in range(ITERS):
        vectors = (inverse_root * panel).astype(BF)
        vsend[t] = vectors
        vrow[t, c] = vectors
        vcol[t, r] = vectors
        own = vsend.at[t]
        cps_h = send(own, vrow.at[t, c], r, col_of(1 - h, e))
        cps_l = [
            send(own, vcol.at[t, r], row_of(y, (l + d) % NL), c) for d in range(1, NL)
        ]
        cps_e = [
            send(own, vrow.at[t, c], r, col_of(h, (e + d) % rest)) for d in range(1, rest)
        ]
        cps_y = [
            send(own, vcol.at[t, r], row_of((y + d) % NY, l), c) for d in range(1, NY)
        ]
        if t > 0:
            gram_local(t, panel)
            gram_cps = gram_start(t)
        for d in range(1, NL):
            cps_l[d - 1].wait_recv()
            got = vcol.at[t, row_of(y, (l - d + NL) % NL)]
            for f in range(1, NY):
                cps_y.append(send(got, got, row_of((y + f) % NY, l), c))
        cps_h.wait_recv()
        got = vrow.at[t, col_of(1 - h, e)]
        cps_far = [send(got, got, r, col_of(h, (e + d) % rest)) for d in range(1, rest)]
        if t > 0:
            gram_cps = gram_y(t, gram_cps)

        wait_all(cps_e)
        near = jnp.concatenate([vrow[t, h * rest + i] for i in range(rest)], axis=1)

        def mirror_near(j, _):
            cols = pl.ds(pl.multiple_of(j * pair, pair), pair)
            out = jnp.dot(
                near,
                matrix[pl.ds(pl.multiple_of(h * half, half), half), cols],
                preferred_element_type=F32,
            )
            msum[t, j // 2, 2 * (j % 2)] = out[:, :B]
            msum[t, j // 2, 2 * (j % 2) + 1] = out[:, B:]
            return 0

        lax.fori_loop(0, 8, mirror_near, 0)
        own_y = jnp.concatenate([vcol[t, y * NL + i] for i in range(NL)], axis=1)

        def direct_near(j, _):
            rows = pl.ds(pl.multiple_of(j * pair, pair), pair)
            out = lax.dot_general(
                own_y,
                matrix[rows, pl.ds(pl.multiple_of(y * quarter, quarter), quarter)],
                (((1,), (1,)), ((), ())),
                preferred_element_type=F32,
            )
            dsum[t, 0, j % 4, j // 4] = out[:, :B]
            dsum[t, 1, j % 4, j // 4] = out[:, B:]
            return 0

        lax.fori_loop(0, 8, direct_near, 0)
        if t > 0:
            gram_cps = gram_z(t, gram_cps)
        wait_all(cps_y)
        others = []
        for d in range(1, NY):
            yy = (y + d) % NY
            others.append(
                (yy, jnp.concatenate([vcol[t, yy * NL + i] for i in range(NL)], axis=1))
            )

        def direct_far(j, _):
            rows = pl.ds(pl.multiple_of(j * pair, pair), pair)
            out = 0.0
            for yy, values in others:
                out = out + lax.dot_general(
                    values,
                    matrix[rows, pl.ds(pl.multiple_of(yy * quarter, quarter), quarter)],
                    (((1,), (1,)), ((), ())),
                    preferred_element_type=F32,
                )
            dsum[t, 0, j % 4, j // 4] += out[:, :B]
            dsum[t, 1, j % 4, j // 4] += out[:, B:]
            return 0

        lax.fori_loop(0, 8, direct_far, 0)
        cps_c = rs_core(dsum.at[t], rc.at[t])
        wait_all(cps_far)
        far = jnp.concatenate([vrow[t, (1 - h) * rest + i] for i in range(rest)], axis=1)

        def mirror_far(j, _):
            cols = pl.ds(pl.multiple_of(j * pair, pair), pair)
            out = jnp.dot(
                far,
                matrix[pl.ds(pl.multiple_of((1 - h) * half, half), half), cols],
                preferred_element_type=F32,
            )
            msum[t, j // 2, 2 * (j % 2)] += out[:, :B]
            msum[t, j // 2, 2 * (j % 2) + 1] += out[:, B:]
            return 0

        lax.fori_loop(0, 8, mirror_far, 0)
        cps_r = ring_start(msum.at[t], yq.at[t], y, device_y)
        wait_all(cps_c)
        d1[t] = dsum[t, core] + rc[t]
        cps_c = ring_start(d1.at[t], xq.at[t], x, device_x)
        if t > 0:
            gram_cps = gram_all(t, gram_cps)
        cps_c = ring_mid(cps_c, d1.at[t], xq.at[t], xm.at[t], x, device_x)
        cps_r = ring_mid(cps_r, msum.at[t], yq.at[t], ym.at[t], y, device_y)
        ring_end(cps_c, d1.at[t], xq.at[t], x, d2.at[t])
        cps_c = rs_h(d2.at[t], rz.at[t])
        ring_end(cps_r, msum.at[t], yq.at[t], y, m1.at[t])
        cps_r = rs_l(m1.at[t], rl.at[t])
        if t > 0:
            factor = gram_end(t, gram_cps)
        wait_all(cps_r)
        wait_all(cps_c)
        product = (d2[t, h] + rz[t]) + (((m1[t, l] + rl[t, 0]) + rl[t, 1]) + rl[t, 2])
        panel = panel + inverse_root * product
        if t > 0:
            panel = jnp.dot(factor, panel, precision=HI, preferred_element_type=F32)

    gram_local(ITERS, panel)
    gram_cps = gram_start(ITERS)
    gram_cps = gram_y(ITERS, gram_cps)
    gram_cps = gram_z(ITERS, gram_cps)
    gram_cps = gram_all(ITERS, gram_cps)
    factor = gram_end(ITERS, gram_cps)
    out_ref[...] = jnp.dot(factor, panel, precision=HI, preferred_element_type=F32)
    for cp in pending:
        cp.wait_send()


def copies():
    gram = 7 + 3 + 7 + 7
    degrees = 1 + 3 + 1 + 3 + 3
    scatter = 1 + 6 + 1 + 6 + 3
    gather = 1 + 3 + 7 + 3 + 9 + 7
    return (ITERS + 1) * gram + degrees + ITERS * (scatter + gather)


def local(start_vectors, cluster_order, weights, block_mask):
    vm = pltpu.VMEM
    n = ITERS
    blk = (K, B)
    hblk = (K // 2, B)
    eblk = (8, B)
    scratch = [
        vm(blk, F32),
        vm((1, B), jnp.int32),
        vm((16, 1, 16), jnp.int32),
        vm((16 * B, 16 * B), BF),
        vm((B, B), BF),
        vm((n,) + blk, BF),
        vm((n, 16) + blk, BF),
        vm((n, 16) + blk, BF),
        vm((n, NC, NX, NH) + blk, F32),
        vm((n, NX, NH) + blk, F32),
        vm((n, NH) + blk, F32),
        vm((n, NX, NH) + blk, F32),
        vm((n, 6, NH) + hblk, F32),
        vm((n, 2, NH) + hblk, F32),
        vm((n,) + blk, F32),
        vm((n, NY, NL) + blk, F32),
        vm((n, NL) + blk, F32),
        vm((n, 6, NL) + hblk, F32),
        vm((n, 2, NL) + hblk, F32),
        vm((n, NL - 1) + blk, F32),
        vm((NC, NX, NH) + eblk, F32),
        vm((NX, NH) + eblk, F32),
        vm((NH,) + eblk, F32),
        vm((NX, NH) + eblk, F32),
        vm((NX - 1, NH) + eblk, F32),
        vm(eblk, F32),
        vm((NY, NL) + eblk, F32),
        vm((NL,) + eblk, F32),
        vm((NY - 1, NL) + eblk, F32),
        vm((NL - 1,) + eblk, F32),
        vm((n + 1, 8) + eblk, F32),
        vm((n + 1, 7) + eblk, F32),
        vm((n + 1,) + eblk, F32),
        vm((n + 1, 3) + eblk, F32),
        vm((n + 1,) + eblk, F32),
        vm((n + 1, 7) + eblk, F32),
        vm((n + 1, 8) + eblk, F32),
        pltpu.SemaphoreType.DMA((20,)),
        pltpu.SemaphoreType.DMA((copies(),)),
        pltpu.SemaphoreType.DMA((copies(),)),
    ]
    hbm = pl.BlockSpec(memory_space=pltpu.HBM)
    panel = pl.pallas_call(
        kernel,
        out_shape=jax.ShapeDtypeStruct(blk, F32),
        in_specs=[hbm] * 4,
        out_specs=pl.BlockSpec(memory_space=pltpu.VMEM),
        scratch_shapes=scratch,
        compiler_params=pltpu.CompilerParams(
            collective_id=0, has_side_effects=True, vmem_limit_bytes=66 * 1000 * 1000
        ),
    )(start_vectors, cluster_order, block_mask, weights[:, 0, :])
    return math.sqrt(16 * 16 * B) * panel


def solution(mesh):
    placed = (
        P(None, ("row", "col")),
        P(("row", "col"), None),
        P("row", "col", None),
        P("row", "col", None),
    )
    return jax.shard_map(
        local, mesh=mesh, in_specs=placed, out_specs=P(None, ("row", "col")), check_vma=False
    )
```

```python
import functools
import math

import jax
import jax.numpy as jnp
from jax import lax
from jax.experimental import pallas as pl
from jax.experimental.pallas import tpu as pltpu
from jax.sharding import PartitionSpec as P

ITERS = 3
K = 64
B = 128
GROUP = 4
STEP = 8
NY, NL, NH, NX, NC = 4, 4, 2, 4, 2
MESH = pl.DeviceIdType.MESH
HI = lax.Precision.HIGHEST
F32 = jnp.float32
BF = jnp.bfloat16


def inverse_factor(blocks):
    groups = K // 8
    lane = lax.broadcasted_iota(jnp.int32, (8, 2 * K), 1)
    sub = lax.broadcasted_iota(jnp.int32, (8, 2 * K), 0)
    rows = [
        jnp.where(lane < K, (lane == sub + 8 * g).astype(F32), blocks[g]) for g in range(groups)
    ]

    def row_of_all(value, k):
        return jnp.broadcast_to(value[k : k + 1, :], (8, 2 * K))

    def column_of_all(value, j):
        return jnp.broadcast_to(value[:, K + j : K + j + 1], (8, 2 * K))

    out = []
    for b in range(groups):
        block = rows[b]
        columns = [column_of_all(block, 8 * b + m) for m in range(8)]
        pivots = {(k, m): row_of_all(columns[m], k) for m in range(8) for k in range(m, 8)}
        lower, inverses, reduced = {}, [], []
        for m in range(8):
            inverses.append(1.0 / pivots[m, m])
            for k in range(m + 1, 8):
                lower[k, m] = pivots[k, m] * inverses[m]
            for k in range(m + 1, 8):
                for n in range(m + 1, k + 1):
                    pivots[k, n] = pivots[k, n] - lower[k, m] * pivots[n, m]
        for k in range(8):
            value = row_of_all(block, k)
            for m in range(k):
                value = value - lower[k, m] * reduced[m]
            reduced.append(value)
        if b + 1 < groups:
            solved = [None] * 8
            for k in reversed(range(8)):
                value = reduced[k] * inverses[k]
                for n in range(k + 1, 8):
                    value = value - lower[n, k] * solved[n]
                solved[k] = value
            for g in range(b + 1, groups):
                value = rows[g]
                for k in range(8):
                    value = value - column_of_all(rows[g], 8 * b + k) * solved[k]
                rows[g] = value
        result = jnp.zeros((8, 2 * K), F32)
        for k in range(8):
            result = jnp.where(sub == k, reduced[k] * (1.0 / jnp.sqrt(pivots[k, k])), result)
        out.append(result)
    return jnp.concatenate(out, axis=0)[:, :K]


def kernel(
    start_hbm,
    order_hbm,
    mask_hbm,
    w_ref,
    out_ref,
    start_ref,
    order_ref,
    mask_ref,
    matrix,
    wdiag,
    vsend,
    vrow,
    vcol,
    dsum,
    d1,
    d2,
    rc,
    xq,
    xm,
    rz,
    msum,
    m1,
    yq,
    ym,
    rl,
    edsum,
    ed1,
    ed2,
    erc,
    erx,
    erz,
    emsum,
    em1,
    ery,
    erl,
    gs,
    ga,
    g1,
    gy,
    g2,
    gz,
    gf,
    wsem,
    ssem,
    rsem,
):
    r = lax.axis_index("row")
    c = lax.axis_index("col")
    y, l = r // NL, r % NL
    h, e = c // (NX * NC), c % (NX * NC)
    x, core = e // NC, e % NC
    z = h * NL + l
    rest = NX * NC

    def col_of(hh, ee):
        return hh * rest + ee

    def row_of(yy, ll):
        return yy * NL + ll

    barrier = pltpu.get_barrier_semaphore()
    for d in range(1, NH * NL):
        zz = (z + d) % (NH * NL)
        pl.semaphore_signal(
            barrier,
            inc=1,
            device_id=(row_of(y, zz % NL), col_of(zz // NL, e)),
            device_id_type=MESH,
        )
    for d in range(1, NY):
        pl.semaphore_signal(
            barrier, inc=1, device_id=(row_of((y + d) % NY, l), c), device_id_type=MESH
        )
    for d in range(1, rest):
        pl.semaphore_signal(
            barrier, inc=1, device_id=(r, col_of(h, (e + d) % rest)), device_id_type=MESH
        )

    local_copies = []
    for i, (src, dst) in enumerate(
        ((order_hbm, order_ref), (start_hbm, start_ref), (mask_hbm, mask_ref))
    ):
        cp = pltpu.make_async_copy(src, dst, wsem.at[17 + i])
        cp.start()
        local_copies.append(cp)
    chunk_copies = []
    for a in range(16):
        cp = pltpu.make_async_copy(
            w_ref.at[pl.ds(a * B, B), :], matrix.at[pl.ds(a * B, B), :], wsem.at[a]
        )
        cp.start()
        chunk_copies.append(cp)
    diag_copy = pltpu.make_async_copy(
        w_ref.at[pl.ds(pl.multiple_of(c * B, B), B), pl.ds(pl.multiple_of(r * B, B), B)],
        wdiag,
        wsem.at[16],
    )
    diag_copy.start()

    count = [0]
    pending = []

    def send(src, dst, row, col):
        index = count[0]
        count[0] += 1
        cp = pltpu.make_async_remote_copy(
            src_ref=src,
            dst_ref=dst,
            send_sem=ssem.at[index],
            recv_sem=rsem.at[index],
            device_id=(row, col),
            device_id_type=MESH,
        )
        cp.start()
        pending.append(cp)
        return cp

    def wait_all(cps):
        for cp in cps:
            cp.wait_recv()

    def gram_local(t, panel):
        padded = jnp.concatenate([jnp.zeros((K, B), F32), panel], axis=0)
        gram = lax.dot_general(
            panel, padded, (((1,), (1,)), ((), ())), precision=HI, preferred_element_type=F32
        )
        for g in range(8):
            gs[t, g] = gram[8 * g : 8 * g + 8]

    def gram_start(t):
        return [
            send(gs.at[t, (e + d) % rest], ga.at[t, d - 1], r, col_of(h, (e + d) % rest))
            for d in range(1, rest)
        ]

    def gram_y(t, cps):
        wait_all(cps)
        total = gs[t, e]
        for d in range(rest - 1):
            total = total + ga[t, d]
        g1[t] = total
        return [
            send(g1.at[t], gy.at[t, d - 1], row_of((y + d) % NY, l), c) for d in range(1, NY)
        ]

    def gram_z(t, cps):
        wait_all(cps)
        g2[t] = ((g1[t] + gy[t, 0]) + gy[t, 1]) + gy[t, 2]
        out = []
        for d in range(1, NH * NL):
            zz = (z + d) % (NH * NL)
            out.append(send(g2.at[t], gz.at[t, d - 1], row_of(y, zz % NL), col_of(zz // NL, e)))
        return out

    def gram_all(t, cps):
        wait_all(cps)
        total = g2[t]
        for d in range(NH * NL - 1):
            total = total + gz[t, d]
        gf[t, e] = total
        return [
            send(gf.at[t, e], gf.at[t, e], r, col_of(h, (e + d) % rest)) for d in range(1, rest)
        ]

    def gram_end(t, cps):
        wait_all(cps)
        return inverse_factor([gf[t, g] for g in range(8)])

    def rs_core(src, dst):
        return [send(src.at[1 - core], dst, r, col_of(h, x * NC + 1 - core))]

    def rs_h(last, dst):
        return [send(last.at[1 - h], dst, r, col_of(1 - h, e))]

    def rs_l(mid, dst):
        out = []
        for d in range(1, NL):
            ll = (l + d) % NL
            out.append(send(mid.at[ll], dst.at[d - 1], row_of(y, ll), c))
        return out

    first, second = pl.ds(0, K // 2), pl.ds(K // 2, K // 2)

    def ring_start(src, q, p, device):
        ahead, behind, across = (p + 1) % 4, (p + 3) % 4, (p + 2) % 4
        return [
            send(src.at[across, :, first, :], q.at[0], *device(ahead)),
            send(src.at[across, :, second, :], q.at[1], *device(behind)),
            send(src.at[ahead, :, second, :], q.at[2], *device(ahead)),
            send(src.at[behind, :, first, :], q.at[3], *device(behind)),
        ]

    def ring_mid(cps, src, q, mid, p, device):
        ahead, behind = (p + 1) % 4, (p + 3) % 4
        cps[0].wait_recv()
        mid[0] = src[ahead, :, first, :] + q[0]
        forth = send(mid.at[0], q.at[4], *device(ahead))
        cps[1].wait_recv()
        mid[1] = src[behind, :, second, :] + q[1]
        back = send(mid.at[1], q.at[5], *device(behind))
        return cps[2:] + [forth, back]

    def ring_end(cps, src, q, p, dst):
        wait_all(cps)
        dst[:, first, :] = (src[p, :, first, :] + q[3]) + q[4]
        dst[:, second, :] = (src[p, :, second, :] + q[2]) + q[5]

    def device_x(p):
        return r, col_of(h, p * NC + core)

    def device_y(p):
        return row_of(p, l), c

    local_copies[0].wait()
    local_copies[1].wait()
    pick = (
        lax.broadcasted_iota(jnp.int32, (B, B), 0) == jnp.broadcast_to(order_ref[...], (B, B))
    ).astype(F32)
    panel = jnp.dot(start_ref[...], pick, precision=HI, preferred_element_type=F32)
    gram_local(0, panel)

    local_copies[2].wait()
    mask = jnp.concatenate([mask_ref[a] for a in range(16)], axis=0)
    spread = (
        lax.broadcasted_iota(jnp.int32, (16, 16 * B), 1) // B
        == lax.broadcasted_iota(jnp.int32, (16, 16 * B), 0)
    ).astype(F32)
    live = jnp.dot((mask > 0).astype(F32), spread, preferred_element_type=F32)
    col_block = lax.broadcasted_iota(jnp.int32, (1, 16 * B), 1) // B * 16 + c
    ones_wide = jnp.ones((8, 16 * B), BF)
    ones_rows = jnp.ones((8, GROUP * B), BF)
    col_totals = jnp.zeros((8, 16 * B), F32)
    group = GROUP
    for a in range(0, 16, group):
        for i in range(group):
            chunk_copies[a + i].wait()
        keep = jnp.concatenate(
            [
                jnp.broadcast_to(
                    jnp.where(
                        (live[a + i : a + i + 1, :] > 0.5) & (col_block > r * 16 + a + i), 1.0, 0.0
                    ).astype(BF),
                    (B, 16 * B),
                )
                for i in range(group)
            ],
            axis=0,
        )
        rows = pl.ds(a * B, group * B)
        block = matrix[rows, :] * keep
        matrix[rows, :] = block
        col_totals = col_totals + jnp.dot(ones_rows, block, preferred_element_type=F32)
        totals = lax.dot_general(
            ones_wide, block, (((1,), (1,)), ((), ())), preferred_element_type=F32
        )
        for i in range(group):
            edsum[(a + i) % 2, (a + i) // 2 % 4, (a + i) // 8] = totals[:, i * B : (i + 1) * B]
        if a == 0:
            pl.semaphore_wait(barrier, NH * NL - 1 + NY - 1 + rest - 1)
            gram_cps = gram_start(0)
    for i in range(16):
        emsum[i // NL, i % NL] = col_totals[:, i * B : (i + 1) * B]
    diag_copy.wait()
    upper = lax.broadcasted_iota(jnp.int32, (B, B), 0) < lax.broadcasted_iota(jnp.int32, (B, B), 1)
    diag_value = jnp.where(upper, wdiag[...].astype(F32), 0.0).astype(BF)
    matrix[pl.ds(pl.multiple_of(c * B, B), B), pl.ds(pl.multiple_of(r * B, B), B)] = diag_value
    diag_degree = jnp.dot(ones_rows[:, :B], diag_value, preferred_element_type=F32) + lax.dot_general(
        ones_rows[:, :B], diag_value, (((1,), (1,)), ((), ())), preferred_element_type=F32
    )

    cps_c = rs_core(edsum, erc)
    cps_r = [
        send(emsum.at[(y + d) % NY], ery.at[d - 1], row_of((y + d) % NY, l), c)
        for d in range(1, NY)
    ]
    gram_cps = gram_y(0, gram_cps)
    wait_all(cps_c)
    ed1[...] = edsum[core] + erc[...]
    cps_c = [
        send(ed1.at[(x + d) % NX], erx.at[d - 1], *device_x((x + d) % NX)) for d in range(1, NX)
    ]
    wait_all(cps_r)
    em1[...] = ((emsum[y] + ery[0]) + ery[1]) + ery[2]
    cps_r = rs_l(em1, erl)
    gram_cps = gram_z(0, gram_cps)
    wait_all(cps_c)
    ed2[...] = ((ed1[x] + erx[0]) + erx[1]) + erx[2]
    cps_c = rs_h(ed2, erz)
    gram_cps = gram_all(0, gram_cps)
    wait_all(cps_r)
    wait_all(cps_c)
    degree = (ed2[h] + erz[...]) + (((em1[l] + erl[0]) + erl[1]) + erl[2]) + diag_degree
    inverse_root = jnp.broadcast_to(1.0 / jnp.sqrt(degree[0:1, :]), (K, B))
    factor = gram_end(0, gram_cps)
    panel = jnp.dot(factor, panel, precision=HI, preferred_element_type=F32)

    half = 8 * B
    quarter = 4 * B
    wide = STEP * B

    for t in range(ITERS):
        vectors = (inverse_root * panel).astype(BF)
        vsend[t] = vectors
        vrow[t, c] = vectors
        vcol[t, r] = vectors
        own = vsend.at[t]
        cps_h = send(own, vrow.at[t, c], r, col_of(1 - h, e))
        cps_l = [
            send(own, vcol.at[t, r], row_of(y, (l + d) % NL), c) for d in range(1, NL)
        ]
        cps_e = [
            send(own, vrow.at[t, c], r, col_of(h, (e + d) % rest)) for d in range(1, rest)
        ]
        cps_y = [
            send(own, vcol.at[t, r], row_of((y + d) % NY, l), c) for d in range(1, NY)
        ]
        if t > 0:
            gram_local(t, panel)
            gram_cps = gram_start(t)
        for d in range(1, NL):
            cps_l[d - 1].wait_recv()
            got = vcol.at[t, row_of(y, (l - d + NL) % NL)]
            for f in range(1, NY):
                cps_y.append(send(got, got, row_of((y + f) % NY, l), c))
        cps_h.wait_recv()
        got = vrow.at[t, col_of(1 - h, e)]
        cps_far = [send(got, got, r, col_of(h, (e + d) % rest)) for d in range(1, rest)]
        if t > 0:
            gram_cps = gram_y(t, gram_cps)

        wait_all(cps_e)
        near = jnp.concatenate([vrow[t, h * rest + i] for i in range(rest)], axis=1)

        def mirror_near(j, _):
            cols = pl.ds(pl.multiple_of(j * wide, wide), wide)
            out = jnp.dot(
                near,
                matrix[pl.ds(pl.multiple_of(h * half, half), half), cols],
                preferred_element_type=F32,
            )
            for i in range(STEP):
                msum[t, j * (STEP // 4) + i // 4, i % 4] = out[:, i * B : (i + 1) * B]
            return 0

        lax.fori_loop(0, 16 // STEP, mirror_near, 0)
        own_y = jnp.concatenate([vcol[t, y * NL + i] for i in range(NL)], axis=1)

        def direct_near(j, _):
            rows = pl.ds(pl.multiple_of(j * wide, wide), wide)
            out = lax.dot_general(
                own_y,
                matrix[rows, pl.ds(pl.multiple_of(y * quarter, quarter), quarter)],
                (((1,), (1,)), ((), ())),
                preferred_element_type=F32,
            )
            for i in range(STEP):
                b = j * STEP + i
                dsum[t, i % 2, b // 2 % 4, b // 8] = out[:, i * B : (i + 1) * B]
            return 0

        lax.fori_loop(0, 16 // STEP, direct_near, 0)
        if t > 0:
            gram_cps = gram_z(t, gram_cps)
        wait_all(cps_y)
        around = [(y + d) % NY for d in range(1, NY)]
        others = jnp.concatenate(
            [vcol[t, yy * NL + i] for yy in around for i in range(NL)], axis=1
        )

        def direct_far(parity):
            stored = jnp.concatenate(
                [
                    jnp.concatenate(
                        [
                            matrix[
                                pl.ds(pl.multiple_of((2 * i + parity) * B, B), B),
                                pl.ds(pl.multiple_of(yy * quarter, quarter), quarter),
                            ]
                            for yy in around
                        ],
                        axis=1,
                    )
                    for i in range(8)
                ],
                axis=0,
            )
            out = lax.dot_general(
                others, stored, (((1,), (1,)), ((), ())), preferred_element_type=F32
            )
            for i in range(8):
                dsum[t, parity, i % 4, i // 4] += out[:, i * B : (i + 1) * B]

        direct_far(1 - core)
        cps_c = rs_core(dsum.at[t], rc.at[t])
        wait_all(cps_far)
        far = jnp.concatenate([vrow[t, (1 - h) * rest + i] for i in range(rest)], axis=1)

        def mirror_far(j, _):
            cols = pl.ds(pl.multiple_of(j * wide, wide), wide)
            out = jnp.dot(
                far,
                matrix[pl.ds(pl.multiple_of((1 - h) * half, half), half), cols],
                preferred_element_type=F32,
            )
            for i in range(STEP):
                msum[t, j * (STEP // 4) + i // 4, i % 4] += out[:, i * B : (i + 1) * B]
            return 0

        lax.fori_loop(0, 16 // STEP, mirror_far, 0)
        cps_r = ring_start(msum.at[t], yq.at[t], y, device_y)
        direct_far(core)
        wait_all(cps_c)
        d1[t] = dsum[t, core] + rc[t]
        cps_c = ring_start(d1.at[t], xq.at[t], x, device_x)
        if t > 0:
            gram_cps = gram_all(t, gram_cps)
        cps_c = ring_mid(cps_c, d1.at[t], xq.at[t], xm.at[t], x, device_x)
        cps_r = ring_mid(cps_r, msum.at[t], yq.at[t], ym.at[t], y, device_y)
        ring_end(cps_c, d1.at[t], xq.at[t], x, d2.at[t])
        cps_c = rs_h(d2.at[t], rz.at[t])
        ring_end(cps_r, msum.at[t], yq.at[t], y, m1.at[t])
        cps_r = rs_l(m1.at[t], rl.at[t])
        if t > 0:
            factor = gram_end(t, gram_cps)
        wait_all(cps_r)
        wait_all(cps_c)
        product = (d2[t, h] + rz[t]) + (((m1[t, l] + rl[t, 0]) + rl[t, 1]) + rl[t, 2])
        panel = panel + inverse_root * product
        if t > 0:
            panel = jnp.dot(factor, panel, precision=HI, preferred_element_type=F32)

    gram_local(ITERS, panel)
    gram_cps = gram_start(ITERS)
    gram_cps = gram_y(ITERS, gram_cps)
    gram_cps = gram_z(ITERS, gram_cps)
    gram_cps = gram_all(ITERS, gram_cps)
    factor = gram_end(ITERS, gram_cps)
    out_ref[...] = jnp.dot(factor, panel, precision=HI, preferred_element_type=F32)
    for cp in pending:
        cp.wait_send()


def copies():
    gram = 7 + 3 + 7 + 7
    degrees = 1 + 3 + 1 + 3 + 3
    scatter = 1 + 6 + 1 + 6 + 3
    gather = 1 + 3 + 7 + 3 + 9 + 7
    return (ITERS + 1) * gram + degrees + ITERS * (scatter + gather)


def local(start_vectors, cluster_order, weights, block_mask):
    vm = pltpu.VMEM
    n = ITERS
    blk = (K, B)
    hblk = (K // 2, B)
    eblk = (8, B)
    scratch = [
        vm(blk, F32),
        vm((1, B), jnp.int32),
        vm((16, 1, 16), jnp.int32),
        vm((16 * B, 16 * B), BF),
        vm((B, B), BF),
        vm((n,) + blk, BF),
        vm((n, 16) + blk, BF),
        vm((n, 16) + blk, BF),
        vm((n, NC, NX, NH) + blk, F32),
        vm((n, NX, NH) + blk, F32),
        vm((n, NH) + blk, F32),
        vm((n, NX, NH) + blk, F32),
        vm((n, 6, NH) + hblk, F32),
        vm((n, 2, NH) + hblk, F32),
        vm((n,) + blk, F32),
        vm((n, NY, NL) + blk, F32),
        vm((n, NL) + blk, F32),
        vm((n, 6, NL) + hblk, F32),
        vm((n, 2, NL) + hblk, F32),
        vm((n, NL - 1) + blk, F32),
        vm((NC, NX, NH) + eblk, F32),
        vm((NX, NH) + eblk, F32),
        vm((NH,) + eblk, F32),
        vm((NX, NH) + eblk, F32),
        vm((NX - 1, NH) + eblk, F32),
        vm(eblk, F32),
        vm((NY, NL) + eblk, F32),
        vm((NL,) + eblk, F32),
        vm((NY - 1, NL) + eblk, F32),
        vm((NL - 1,) + eblk, F32),
        vm((n + 1, 8) + eblk, F32),
        vm((n + 1, 7) + eblk, F32),
        vm((n + 1,) + eblk, F32),
        vm((n + 1, 3) + eblk, F32),
        vm((n + 1,) + eblk, F32),
        vm((n + 1, 7) + eblk, F32),
        vm((n + 1, 8) + eblk, F32),
        pltpu.SemaphoreType.DMA((20,)),
        pltpu.SemaphoreType.DMA((copies(),)),
        pltpu.SemaphoreType.DMA((copies(),)),
    ]
    hbm = pl.BlockSpec(memory_space=pltpu.HBM)
    panel = pl.pallas_call(
        kernel,
        out_shape=jax.ShapeDtypeStruct(blk, F32),
        in_specs=[hbm] * 4,
        out_specs=pl.BlockSpec(memory_space=pltpu.VMEM),
        scratch_shapes=scratch,
        compiler_params=pltpu.CompilerParams(
            collective_id=0, has_side_effects=True, vmem_limit_bytes=66 * 1000 * 1000
        ),
    )(start_vectors, cluster_order, block_mask, weights[:, 0, :])
    return math.sqrt(16 * 16 * B) * panel


def solution(mesh):
    placed = (
        P(None, ("row", "col")),
        P(("row", "col"), None),
        P("row", "col", None),
        P("row", "col", None),
    )
    return jax.shard_map(
        local, mesh=mesh, in_specs=placed, out_specs=P(None, ("row", "col")), check_vma=False
    )
```

```python
import functools
import math

import jax
import jax.numpy as jnp
from jax import lax
from jax.experimental import pallas as pl
from jax.experimental.pallas import tpu as pltpu
from jax.sharding import PartitionSpec as P

ITERS = 3
K = 64
B = 128
GROUP = 4
STEP = 8
FLIP = 256
NY, NL, NH, NX, NC = 4, 4, 2, 4, 2
MESH = pl.DeviceIdType.MESH
HI = lax.Precision.HIGHEST
F32 = jnp.float32
BF = jnp.bfloat16


def inverse_factor(blocks):
    groups = K // 8
    lane = lax.broadcasted_iota(jnp.int32, (8, 2 * K), 1)
    sub = lax.broadcasted_iota(jnp.int32, (8, 2 * K), 0)
    rows = [
        jnp.where(lane < K, (lane == sub + 8 * g).astype(F32), blocks[g]) for g in range(groups)
    ]

    def row_of_all(value, k):
        return jnp.broadcast_to(value[k : k + 1, :], (8, 2 * K))

    def column_of_all(value, j):
        return jnp.broadcast_to(value[:, K + j : K + j + 1], (8, 2 * K))

    out = []
    for b in range(groups):
        block = rows[b]
        columns = [column_of_all(block, 8 * b + m) for m in range(8)]
        pivots = {(k, m): row_of_all(columns[m], k) for m in range(8) for k in range(m, 8)}
        lower, inverses, reduced = {}, [], []
        for m in range(0, 8, 2):
            n = m + 1
            first, cross, second = pivots[m, m], pivots[n, m], pivots[n, n]
            one = 1.0 / first
            two = first * (1.0 / (first * second - cross * cross))
            inverses += [one, two]
            lower[n, m] = cross * one
            pivots[n, n] = second - cross * lower[n, m]
            for k in range(m + 2, 8):
                lower[k, m] = pivots[k, m] * one
                pivots[k, n] = pivots[k, n] - pivots[k, m] * lower[n, m]
                lower[k, n] = pivots[k, n] * two
            for k in range(m + 2, 8):
                for i in range(m + 2, k + 1):
                    pivots[k, i] = (pivots[k, i] - lower[k, m] * pivots[i, m]) - lower[
                        k, n
                    ] * pivots[i, n]
        for k in range(8):
            value = row_of_all(block, k)
            for m in range(k):
                value = value - lower[k, m] * reduced[m]
            reduced.append(value)
        if b + 1 < groups:
            solved = [None] * 8
            for k in reversed(range(8)):
                value = reduced[k] * inverses[k]
                for n in range(k + 1, 8):
                    value = value - lower[n, k] * solved[n]
                solved[k] = value
            for g in range(b + 1, groups):
                value = rows[g]
                for k in range(8):
                    value = value - column_of_all(rows[g], 8 * b + k) * solved[k]
                rows[g] = value
        result = jnp.zeros((8, 2 * K), F32)
        for k in range(8):
            result = jnp.where(sub == k, reduced[k] * (1.0 / jnp.sqrt(pivots[k, k])), result)
        out.append(result)
    return jnp.concatenate(out, axis=0)[:, :K]


def kernel(
    start_hbm,
    order_hbm,
    mask_hbm,
    w_ref,
    out_ref,
    start_ref,
    order_ref,
    mask_ref,
    matrix,
    flipped,
    wdiag,
    vsend,
    vrow,
    vcol,
    dsum,
    d1,
    d2,
    rc,
    xq,
    xm,
    rz,
    msum,
    m1,
    yq,
    ym,
    rl,
    edsum,
    ed1,
    ed2,
    erc,
    erx,
    erz,
    emsum,
    em1,
    ery,
    erl,
    gs,
    ga,
    g1,
    gy,
    g2,
    gz,
    gf,
    wsem,
    ssem,
    rsem,
):
    r = lax.axis_index("row")
    c = lax.axis_index("col")
    y, l = r // NL, r % NL
    h, e = c // (NX * NC), c % (NX * NC)
    x, core = e // NC, e % NC
    z = h * NL + l
    rest = NX * NC

    def col_of(hh, ee):
        return hh * rest + ee

    def row_of(yy, ll):
        return yy * NL + ll

    barrier = pltpu.get_barrier_semaphore()
    for d in range(1, NH * NL):
        zz = (z + d) % (NH * NL)
        pl.semaphore_signal(
            barrier,
            inc=1,
            device_id=(row_of(y, zz % NL), col_of(zz // NL, e)),
            device_id_type=MESH,
        )
    for d in range(1, NY):
        pl.semaphore_signal(
            barrier, inc=1, device_id=(row_of((y + d) % NY, l), c), device_id_type=MESH
        )
    for d in range(1, rest):
        pl.semaphore_signal(
            barrier, inc=1, device_id=(r, col_of(h, (e + d) % rest)), device_id_type=MESH
        )

    local_copies = []
    for i, (src, dst) in enumerate(
        ((order_hbm, order_ref), (start_hbm, start_ref), (mask_hbm, mask_ref))
    ):
        cp = pltpu.make_async_copy(src, dst, wsem.at[17 + i])
        cp.start()
        local_copies.append(cp)
    chunk_copies = []
    for a in range(16):
        cp = pltpu.make_async_copy(
            w_ref.at[pl.ds(a * B, B), :], matrix.at[pl.ds(a * B, B), :], wsem.at[a]
        )
        cp.start()
        chunk_copies.append(cp)
    diag_copy = pltpu.make_async_copy(
        w_ref.at[pl.ds(pl.multiple_of(c * B, B), B), pl.ds(pl.multiple_of(r * B, B), B)],
        wdiag,
        wsem.at[16],
    )
    diag_copy.start()

    count = [0]
    pending = []

    def send(src, dst, row, col):
        index = count[0]
        count[0] += 1
        cp = pltpu.make_async_remote_copy(
            src_ref=src,
            dst_ref=dst,
            send_sem=ssem.at[index],
            recv_sem=rsem.at[index],
            device_id=(row, col),
            device_id_type=MESH,
        )
        cp.start()
        pending.append(cp)
        return cp

    def wait_all(cps):
        for cp in cps:
            cp.wait_recv()

    def gram_local(t, panel):
        padded = jnp.concatenate([jnp.zeros((K, B), F32), panel], axis=0)
        gram = lax.dot_general(
            panel, padded, (((1,), (1,)), ((), ())), precision=HI, preferred_element_type=F32
        )
        for g in range(8):
            gs[t, g] = gram[8 * g : 8 * g + 8]

    def gram_start(t):
        return [
            send(gs.at[t, (e + d) % rest], ga.at[t, d - 1], r, col_of(h, (e + d) % rest))
            for d in range(1, rest)
        ]

    def gram_y(t, cps):
        wait_all(cps)
        total = gs[t, e]
        for d in range(rest - 1):
            total = total + ga[t, d]
        g1[t] = total
        return [
            send(g1.at[t], gy.at[t, d - 1], row_of((y + d) % NY, l), c) for d in range(1, NY)
        ]

    def gram_z(t, cps):
        wait_all(cps)
        g2[t] = ((g1[t] + gy[t, 0]) + gy[t, 1]) + gy[t, 2]
        out = []
        for d in range(1, NH * NL):
            zz = (z + d) % (NH * NL)
            out.append(send(g2.at[t], gz.at[t, d - 1], row_of(y, zz % NL), col_of(zz // NL, e)))
        return out

    def gram_all(t, cps):
        wait_all(cps)
        total = g2[t]
        for d in range(NH * NL - 1):
            total = total + gz[t, d]
        gf[t, e] = total
        return [
            send(gf.at[t, e], gf.at[t, e], r, col_of(h, (e + d) % rest)) for d in range(1, rest)
        ]

    def gram_end(t, cps):
        wait_all(cps)
        return inverse_factor([gf[t, g] for g in range(8)])

    def rs_core(src, dst):
        return [send(src.at[1 - core], dst, r, col_of(h, x * NC + 1 - core))]

    def rs_h(last, dst):
        return [send(last.at[1 - h], dst, r, col_of(1 - h, e))]

    def rs_l(mid, dst):
        out = []
        for d in range(1, NL):
            ll = (l + d) % NL
            out.append(send(mid.at[ll], dst.at[d - 1], row_of(y, ll), c))
        return out

    def ring_start(src, short, q, p, device):
        short[...] = src[...].astype(BF)
        return [
            send(short.at[(p + d) % 4], q.at[d - 1], *device((p + d) % 4)) for d in (2, 1, 3)
        ]

    def ring_end(cps, src, q, p, dst):
        wait_all(cps)
        dst[...] = (src[p] + q[0].astype(F32)) + (q[1].astype(F32) + q[2].astype(F32))

    def device_x(p):
        return r, col_of(h, p * NC + core)

    def device_y(p):
        return row_of(p, l), c

    def flip(part):
        def step(j, _):
            rows = pl.ds(pl.multiple_of(j * FLIP, FLIP), FLIP)
            flipped[:, rows] = matrix[rows, :].T
            return 0

        count = 16 * B // FLIP // 2
        lax.fori_loop(part * count, (part + 1) * count, step, 0)

    local_copies[0].wait()
    local_copies[1].wait()
    pick = (
        lax.broadcasted_iota(jnp.int32, (B, B), 0) == jnp.broadcast_to(order_ref[...], (B, B))
    ).astype(F32)
    panel = jnp.dot(start_ref[...], pick, precision=HI, preferred_element_type=F32)
    gram_local(0, panel)

    local_copies[2].wait()
    mask = jnp.concatenate([mask_ref[a] for a in range(16)], axis=0)
    spread = (
        lax.broadcasted_iota(jnp.int32, (16, 16 * B), 1) // B
        == lax.broadcasted_iota(jnp.int32, (16, 16 * B), 0)
    ).astype(F32)
    live = jnp.dot((mask > 0).astype(F32), spread, preferred_element_type=F32)
    col_block = lax.broadcasted_iota(jnp.int32, (1, 16 * B), 1) // B * 16 + c
    ones_wide = jnp.ones((8, 16 * B), BF)
    ones_rows = jnp.ones((8, GROUP * B), BF)
    col_totals = jnp.zeros((8, 16 * B), F32)
    group = GROUP
    for a in range(0, 16, group):
        for i in range(group):
            chunk_copies[a + i].wait()
        keep = jnp.concatenate(
            [
                jnp.broadcast_to(
                    jnp.where(
                        (live[a + i : a + i + 1, :] > 0.5) & (col_block > r * 16 + a + i), 1.0, 0.0
                    ).astype(BF),
                    (B, 16 * B),
                )
                for i in range(group)
            ],
            axis=0,
        )
        rows = pl.ds(a * B, group * B)
        block = matrix[rows, :] * keep
        matrix[rows, :] = block
        col_totals = col_totals + jnp.dot(ones_rows, block, preferred_element_type=F32)
        totals = lax.dot_general(
            ones_wide, block, (((1,), (1,)), ((), ())), preferred_element_type=F32
        )
        for i in range(group):
            edsum[(a + i) % 2, (a + i) // 2 % 4, (a + i) // 8] = totals[:, i * B : (i + 1) * B]
        if a == 0:
            pl.semaphore_wait(barrier, NH * NL - 1 + NY - 1 + rest - 1)
            gram_cps = gram_start(0)
    for i in range(16):
        emsum[i // NL, i % NL] = col_totals[:, i * B : (i + 1) * B]
    diag_copy.wait()
    upper = lax.broadcasted_iota(jnp.int32, (B, B), 0) < lax.broadcasted_iota(jnp.int32, (B, B), 1)
    diag_value = jnp.where(upper, wdiag[...].astype(F32), 0.0).astype(BF)
    matrix[pl.ds(pl.multiple_of(c * B, B), B), pl.ds(pl.multiple_of(r * B, B), B)] = diag_value
    diag_degree = jnp.dot(ones_rows[:, :B], diag_value, preferred_element_type=F32) + lax.dot_general(
        ones_rows[:, :B], diag_value, (((1,), (1,)), ((), ())), preferred_element_type=F32
    )

    cps_c = rs_core(edsum, erc)
    cps_r = [
        send(emsum.at[(y + d) % NY], ery.at[d - 1], row_of((y + d) % NY, l), c)
        for d in range(1, NY)
    ]
    gram_cps = gram_y(0, gram_cps)
    wait_all(cps_c)
    ed1[...] = edsum[core] + erc[...]
    cps_c = [
        send(ed1.at[(x + d) % NX], erx.at[d - 1], *device_x((x + d) % NX)) for d in range(1, NX)
    ]
    flip(0)
    wait_all(cps_r)
    em1[...] = ((emsum[y] + ery[0]) + ery[1]) + ery[2]
    cps_r = rs_l(em1, erl)
    gram_cps = gram_z(0, gram_cps)
    flip(1)
    wait_all(cps_c)
    ed2[...] = ((ed1[x] + erx[0]) + erx[1]) + erx[2]
    cps_c = rs_h(ed2, erz)
    gram_cps = gram_all(0, gram_cps)
    wait_all(cps_r)
    wait_all(cps_c)
    degree = (ed2[h] + erz[...]) + (((em1[l] + erl[0]) + erl[1]) + erl[2]) + diag_degree
    inverse_root = jnp.broadcast_to(1.0 / jnp.sqrt(degree[0:1, :]), (K, B))
    factor = gram_end(0, gram_cps)
    panel = jnp.dot(factor, panel, precision=HI, preferred_element_type=F32)

    half = 8 * B
    wide = STEP * B

    for t in range(ITERS):
        vectors = (inverse_root * panel).astype(BF)
        vsend[t] = vectors
        vrow[t, c] = vectors
        vcol[t, r] = vectors
        own = vsend.at[t]
        cps_h = send(own, vrow.at[t, c], r, col_of(1 - h, e))
        cps_l = [
            send(own, vcol.at[t, r], row_of(y, (l + d) % NL), c) for d in range(1, NL)
        ]
        cps_e = [
            send(own, vrow.at[t, c], r, col_of(h, (e + d) % rest)) for d in range(1, rest)
        ]
        cps_y = [
            send(own, vcol.at[t, r], row_of((y + d) % NY, l), c) for d in range(1, NY)
        ]
        if t > 0:
            gram_local(t, panel)
            gram_cps = gram_start(t)
        for d in range(1, NL):
            cps_l[d - 1].wait_recv()
            got = vcol.at[t, row_of(y, (l - d + NL) % NL)]
            for f in range(1, NY):
                cps_y.append(send(got, got, row_of((y + f) % NY, l), c))
        cps_h.wait_recv()
        got = vrow.at[t, col_of(1 - h, e)]
        cps_far = [send(got, got, r, col_of(h, (e + d) % rest)) for d in range(1, rest)]
        if t > 0:
            gram_cps = gram_y(t, gram_cps)

        wait_all(cps_e)
        near = jnp.concatenate([vrow[t, h * rest + i] for i in range(rest)], axis=1)

        def mirror_near(j, _):
            cols = pl.ds(pl.multiple_of(j * wide, wide), wide)
            out = jnp.dot(
                near,
                matrix[pl.ds(pl.multiple_of(h * half, half), half), cols],
                preferred_element_type=F32,
            )
            for i in range(STEP):
                msum[t, j * (STEP // 4) + i // 4, i % 4] = out[:, i * B : (i + 1) * B]
            return 0

        lax.fori_loop(0, 16 // STEP, mirror_near, 0)
        wait_all(cps_y[: NY - 1])
        around = [(y + d) % NY for d in range(1, NY)]
        early = jnp.concatenate(
            [vcol[t, y * NL + i] for i in range(NL)] + [vcol[t, row_of(yy, l)] for yy in around],
            axis=1,
        )

        def stored_rows(blocks, cols):
            return jnp.concatenate(
                [flipped[pl.ds(pl.multiple_of(i * B, B), B), cols] for i in blocks], axis=0
            )

        def direct_near(j, _):
            cols = pl.ds(pl.multiple_of(j * wide, wide), wide)
            out = jnp.dot(
                early,
                stored_rows([y * NL + i for i in range(NL)] + [row_of(yy, l) for yy in around], cols),
                preferred_element_type=F32,
            )
            for i in range(STEP):
                b = j * STEP + i
                dsum[t, i % 2, b // 2 % 4, b // 8] = out[:, i * B : (i + 1) * B]
            return 0

        lax.fori_loop(0, 16 // STEP, direct_near, 0)
        def forwarded(d):
            return [row_of(yy, (l + NL - d) % NL) for yy in around]

        wait_all(cps_y[NY - 1 : 2 * (NY - 1)])
        middle = jnp.concatenate([vcol[t, i] for i in forwarded(1)], axis=1)

        def direct_middle(j, _):
            cols = pl.ds(pl.multiple_of(j * wide, wide), wide)
            out = jnp.dot(middle, stored_rows(forwarded(1), cols), preferred_element_type=F32)
            for i in range(STEP):
                b = j * STEP + i
                dsum[t, i % 2, b // 2 % 4, b // 8] += out[:, i * B : (i + 1) * B]
            return 0

        lax.fori_loop(0, 16 // STEP, direct_middle, 0)
        wait_all(cps_y[2 * (NY - 1) :])
        late = forwarded(2) + forwarded(3)
        others = jnp.concatenate([vcol[t, i] for i in late], axis=1)

        def direct_far(parity):
            stored = jnp.concatenate(
                [
                    stored_rows(late, pl.ds(pl.multiple_of((2 * i + parity) * B, B), B))
                    for i in range(8)
                ],
                axis=1,
            )
            out = jnp.dot(others, stored, preferred_element_type=F32)
            for i in range(8):
                dsum[t, parity, i % 4, i // 4] += out[:, i * B : (i + 1) * B]

        direct_far(1 - core)
        cps_c = rs_core(dsum.at[t], rc.at[t])
        wait_all(cps_far)
        far = jnp.concatenate([vrow[t, (1 - h) * rest + i] for i in range(rest)], axis=1)

        def mirror_far(j, _):
            cols = pl.ds(pl.multiple_of(j * wide, wide), wide)
            out = jnp.dot(
                far,
                matrix[pl.ds(pl.multiple_of((1 - h) * half, half), half), cols],
                preferred_element_type=F32,
            )
            for i in range(STEP):
                msum[t, j * (STEP // 4) + i // 4, i % 4] += out[:, i * B : (i + 1) * B]
            return 0

        lax.fori_loop(0, 16 // STEP, mirror_far, 0)
        cps_r = ring_start(msum.at[t], ym.at[t], yq.at[t], y, device_y)
        if t > 0:
            gram_cps = gram_z(t, gram_cps)
        direct_far(core)
        wait_all(cps_c)
        d1[t] = dsum[t, core] + rc[t]
        cps_c = ring_start(d1.at[t], xm.at[t], xq.at[t], x, device_x)
        ring_end(cps_c, d1.at[t], xq.at[t], x, d2.at[t])
        cps_c = rs_h(d2.at[t], rz.at[t])
        ring_end(cps_r, msum.at[t], yq.at[t], y, m1.at[t])
        cps_r = rs_l(m1.at[t], rl.at[t])
        if t > 0:
            gram_cps = gram_all(t, gram_cps)
        if t > 0:
            factor = gram_end(t, gram_cps)
        wait_all(cps_r)
        wait_all(cps_c)
        product = (d2[t, h] + rz[t]) + (((m1[t, l] + rl[t, 0]) + rl[t, 1]) + rl[t, 2])
        panel = panel + inverse_root * product
        if t > 0:
            panel = jnp.dot(factor, panel, precision=HI, preferred_element_type=F32)

    gram_local(ITERS, panel)
    gram_cps = gram_start(ITERS)
    done = len(pending)
    for cp in pending[: done - 7]:
        cp.wait_send()
    del pending[: done - 7]
    gram_cps = gram_y(ITERS, gram_cps)
    gram_cps = gram_z(ITERS, gram_cps)
    gram_cps = gram_all(ITERS, gram_cps)
    factor = gram_end(ITERS, gram_cps)
    out_ref[...] = jnp.dot(factor, panel, precision=HI, preferred_element_type=F32)
    for cp in pending:
        cp.wait_send()


def copies():
    gram = 7 + 3 + 7 + 7
    degrees = 1 + 3 + 1 + 3 + 3
    scatter = 1 + 3 + 1 + 3 + 3
    gather = 1 + 3 + 7 + 3 + 9 + 7
    return (ITERS + 1) * gram + degrees + ITERS * (scatter + gather)


def local(start_vectors, cluster_order, weights, block_mask):
    vm = pltpu.VMEM
    n = ITERS
    blk = (K, B)
    eblk = (8, B)
    scratch = [
        vm(blk, F32),
        vm((1, B), jnp.int32),
        vm((16, 1, 16), jnp.int32),
        vm((16 * B, 16 * B), BF),
        vm((16 * B, 16 * B), BF),
        vm((B, B), BF),
        vm((n,) + blk, BF),
        vm((n, 16) + blk, BF),
        vm((n, 16) + blk, BF),
        vm((n, NC, NX, NH) + blk, F32),
        vm((n, NX, NH) + blk, F32),
        vm((n, NH) + blk, F32),
        vm((n, NX, NH) + blk, F32),
        vm((n, NX - 1, NH) + blk, BF),
        vm((n, NX, NH) + blk, BF),
        vm((n,) + blk, F32),
        vm((n, NY, NL) + blk, F32),
        vm((n, NL) + blk, F32),
        vm((n, NY - 1, NL) + blk, BF),
        vm((n, NY, NL) + blk, BF),
        vm((n, NL - 1) + blk, F32),
        vm((NC, NX, NH) + eblk, F32),
        vm((NX, NH) + eblk, F32),
        vm((NH,) + eblk, F32),
        vm((NX, NH) + eblk, F32),
        vm((NX - 1, NH) + eblk, F32),
        vm(eblk, F32),
        vm((NY, NL) + eblk, F32),
        vm((NL,) + eblk, F32),
        vm((NY - 1, NL) + eblk, F32),
        vm((NL - 1,) + eblk, F32),
        vm((n + 1, 8) + eblk, F32),
        vm((n + 1, 7) + eblk, F32),
        vm((n + 1,) + eblk, F32),
        vm((n + 1, 3) + eblk, F32),
        vm((n + 1,) + eblk, F32),
        vm((n + 1, 7) + eblk, F32),
        vm((n + 1, 8) + eblk, F32),
        pltpu.SemaphoreType.DMA((20,)),
        pltpu.SemaphoreType.DMA((copies(),)),
        pltpu.SemaphoreType.DMA((copies(),)),
    ]
    hbm = pl.BlockSpec(memory_space=pltpu.HBM)
    panel = pl.pallas_call(
        kernel,
        out_shape=jax.ShapeDtypeStruct(blk, F32),
        in_specs=[hbm] * 4,
        out_specs=pl.BlockSpec(memory_space=pltpu.VMEM),
        scratch_shapes=scratch,
        compiler_params=pltpu.CompilerParams(
            collective_id=0, has_side_effects=True, vmem_limit_bytes=50 * 1000 * 1000
        ),
    )(
        *[
            pltpu.with_memory_space_constraint(v, pltpu.HBM)
            for v in (start_vectors, cluster_order, block_mask, weights[:, 0, :])
        ]
    )
    return math.sqrt(16 * 16 * B) * panel


def solution(mesh):
    placed = (
        P(None, ("row", "col")),
        P(("row", "col"), None),
        P("row", "col", None),
        P("row", "col", None),
    )
    return jax.shard_map(
        local, mesh=mesh, in_specs=placed, out_specs=P(None, ("row", "col")), check_vma=False
    )
```

```python
import functools
import math

import jax
import jax.numpy as jnp
from jax import lax
from jax.experimental import pallas as pl
from jax.experimental.pallas import tpu as pltpu
from jax.sharding import PartitionSpec as P

ITERS = 3
K = 64
B = 128
GROUP = 4
STEP = 8
FLIP = 256
NY, NL, NH, NX, NC = 4, 4, 2, 4, 2
MESH = pl.DeviceIdType.MESH
HI = lax.Precision.HIGHEST
F32 = jnp.float32
BF = jnp.bfloat16


def inverse_factor(blocks):
    groups = K // 8
    lane = lax.broadcasted_iota(jnp.int32, (8, 2 * K), 1)
    sub = lax.broadcasted_iota(jnp.int32, (8, 2 * K), 0)
    rows = [
        jnp.where(lane < K, (lane == sub + 8 * g).astype(F32), blocks[g]) for g in range(groups)
    ]

    def row_of_all(value, k):
        return jnp.broadcast_to(value[k : k + 1, :], (8, 2 * K))

    def column_of_all(value, j):
        return jnp.broadcast_to(value[:, K + j : K + j + 1], (8, 2 * K))

    out = []
    for b in range(groups):
        block = rows[b]
        columns = [column_of_all(block, 8 * b + m) for m in range(8)]
        pivots = {(k, m): row_of_all(columns[m], k) for m in range(8) for k in range(m, 8)}
        lower, inverses, reduced = {}, [], []
        for m in range(0, 8, 2):
            n = m + 1
            first, cross, second = pivots[m, m], pivots[n, m], pivots[n, n]
            one = 1.0 / first
            two = first * (1.0 / (first * second - cross * cross))
            inverses += [one, two]
            lower[n, m] = cross * one
            pivots[n, n] = second - cross * lower[n, m]
            for k in range(m + 2, 8):
                lower[k, m] = pivots[k, m] * one
                pivots[k, n] = pivots[k, n] - pivots[k, m] * lower[n, m]
                lower[k, n] = pivots[k, n] * two
            for k in range(m + 2, 8):
                for i in range(m + 2, k + 1):
                    pivots[k, i] = (pivots[k, i] - lower[k, m] * pivots[i, m]) - lower[
                        k, n
                    ] * pivots[i, n]
        for k in range(8):
            value = row_of_all(block, k)
            for m in range(k):
                value = value - lower[k, m] * reduced[m]
            reduced.append(value)
        if b + 1 < groups:
            solved = [None] * 8
            for k in reversed(range(8)):
                value = reduced[k] * inverses[k]
                for n in range(k + 1, 8):
                    value = value - lower[n, k] * solved[n]
                solved[k] = value
            for g in range(b + 1, groups):
                value = rows[g]
                for k in range(8):
                    value = value - column_of_all(rows[g], 8 * b + k) * solved[k]
                rows[g] = value
        result = jnp.zeros((8, 2 * K), F32)
        for k in range(8):
            result = jnp.where(sub == k, reduced[k] * (1.0 / jnp.sqrt(pivots[k, k])), result)
        out.append(result)
    return jnp.concatenate(out, axis=0)[:, :K]


def kernel(
    start_hbm,
    order_hbm,
    mask_hbm,
    w_ref,
    out_ref,
    start_ref,
    order_ref,
    mask_ref,
    matrix,
    flipped,
    wdiag,
    vsend,
    vrow,
    vcol,
    dsum,
    d1,
    d2,
    d3,
    rc,
    xq,
    xm,
    rz,
    msum,
    m1,
    m2,
    yq,
    ym,
    rl,
    edsum,
    ed1,
    ed2,
    erc,
    erx,
    erz,
    emsum,
    em1,
    ery,
    erl,
    gs,
    ga,
    g1,
    gy,
    g2,
    gz,
    gf,
    wsem,
    ssem,
    rsem,
):
    r = lax.axis_index("row")
    c = lax.axis_index("col")
    y, l = r // NL, r % NL
    h, e = c // (NX * NC), c % (NX * NC)
    x, core = e // NC, e % NC
    z = h * NL + l
    rest = NX * NC

    def col_of(hh, ee):
        return hh * rest + ee

    def row_of(yy, ll):
        return yy * NL + ll

    barrier = pltpu.get_barrier_semaphore()
    for d in range(1, NH * NL):
        zz = (z + d) % (NH * NL)
        pl.semaphore_signal(
            barrier,
            inc=1,
            device_id=(row_of(y, zz % NL), col_of(zz // NL, e)),
            device_id_type=MESH,
        )
    for d in range(1, NY):
        pl.semaphore_signal(
            barrier, inc=1, device_id=(row_of((y + d) % NY, l), c), device_id_type=MESH
        )
    for d in range(1, rest):
        pl.semaphore_signal(
            barrier, inc=1, device_id=(r, col_of(h, (e + d) % rest)), device_id_type=MESH
        )

    local_copies = []
    for i, (src, dst) in enumerate(
        ((order_hbm, order_ref), (start_hbm, start_ref), (mask_hbm, mask_ref))
    ):
        cp = pltpu.make_async_copy(src, dst, wsem.at[17 + i])
        cp.start()
        local_copies.append(cp)
    chunk_copies = []
    for a in range(16):
        cp = pltpu.make_async_copy(
            w_ref.at[pl.ds(a * B, B), :], matrix.at[pl.ds(a * B, B), :], wsem.at[a]
        )
        cp.start()
        chunk_copies.append(cp)
    diag_copy = pltpu.make_async_copy(
        w_ref.at[pl.ds(pl.multiple_of(c * B, B), B), pl.ds(pl.multiple_of(r * B, B), B)],
        wdiag,
        wsem.at[16],
    )
    diag_copy.start()

    count = [0]
    pending = []

    def send(src, dst, row, col):
        index = count[0]
        count[0] += 1
        cp = pltpu.make_async_remote_copy(
            src_ref=src,
            dst_ref=dst,
            send_sem=ssem.at[index],
            recv_sem=rsem.at[index],
            device_id=(row, col),
            device_id_type=MESH,
        )
        cp.start()
        pending.append(cp)
        return cp

    def wait_all(cps):
        for cp in cps:
            cp.wait_recv()

    def gram_local(t, panel):
        padded = jnp.concatenate([jnp.zeros((K, B), F32), panel], axis=0)
        gram = lax.dot_general(
            panel, padded, (((1,), (1,)), ((), ())), precision=HI, preferred_element_type=F32
        )
        for g in range(8):
            gs[t, g] = gram[8 * g : 8 * g + 8]

    def gram_start(t):
        return [
            send(gs.at[t, (e + d) % rest], ga.at[t, d - 1], r, col_of(h, (e + d) % rest))
            for d in range(1, rest)
        ]

    def gram_z(t, cps):
        wait_all(cps)
        total = gs[t, e]
        for d in range(rest - 1):
            total = total + ga[t, d]
        g1[t] = total
        out = []
        for d in range(1, NH * NL):
            zz = (z + d) % (NH * NL)
            out.append(send(g1.at[t], gz.at[t, d - 1], row_of(y, zz % NL), col_of(zz // NL, e)))
        return out

    def gram_y(t, cps):
        wait_all(cps)
        total = g1[t]
        for d in range(NH * NL - 1):
            total = total + gz[t, d]
        g2[t] = total
        return [
            send(g2.at[t], gy.at[t, d - 1], row_of((y + d) % NY, l), c) for d in range(1, NY)
        ]

    def gram_all(t, cps):
        wait_all(cps)
        gf[t, e] = ((g2[t] + gy[t, 0]) + gy[t, 1]) + gy[t, 2]
        return [
            send(gf.at[t, e], gf.at[t, e], r, col_of(h, (e + d) % rest)) for d in range(1, rest)
        ]

    def gram_end(t, cps):
        wait_all(cps)
        return inverse_factor([gf[t, g] for g in range(8)])

    def rs_core(src, dst):
        return [send(src.at[1 - core], dst, r, col_of(h, x * NC + 1 - core))]

    def rs_h(last, dst):
        return [send(last.at[1 - h], dst, r, col_of(1 - h, e))]

    def rs_l(mid, dst):
        out = []
        for d in range(1, NL):
            ll = (l + d) % NL
            out.append(send(mid.at[ll], dst.at[d - 1], row_of(y, ll), c))
        return out

    def ring_start(src, short, q, p, device):
        short[...] = src[...].astype(BF)
        return [
            send(short.at[(p + d) % 4], q.at[d - 1], *device((p + d) % 4)) for d in (2, 1, 3)
        ]

    def ring_end(cps, src, q, p, dst):
        wait_all(cps)
        dst[...] = (src[p] + q[0].astype(F32)) + (q[1].astype(F32) + q[2].astype(F32))

    def device_x(p):
        return r, col_of(h, p * NC + core)

    def device_y(p):
        return row_of(p, l), c

    def flip(part):
        def step(j, _):
            rows = pl.ds(pl.multiple_of(j * FLIP, FLIP), FLIP)
            flipped[:, rows] = matrix[rows, :].T
            return 0

        count = 16 * B // FLIP // 2
        lax.fori_loop(part * count, (part + 1) * count, step, 0)

    local_copies[0].wait()
    local_copies[1].wait()
    pick = (
        lax.broadcasted_iota(jnp.int32, (B, B), 0) == jnp.broadcast_to(order_ref[...], (B, B))
    ).astype(F32)
    panel = jnp.dot(start_ref[...], pick, precision=HI, preferred_element_type=F32)
    gram_local(0, panel)

    local_copies[2].wait()
    mask = jnp.concatenate([mask_ref[a] for a in range(16)], axis=0)
    spread = (
        lax.broadcasted_iota(jnp.int32, (16, 16 * B), 1) // B
        == lax.broadcasted_iota(jnp.int32, (16, 16 * B), 0)
    ).astype(F32)
    live = jnp.dot((mask > 0).astype(F32), spread, preferred_element_type=F32)
    col_block = lax.broadcasted_iota(jnp.int32, (1, 16 * B), 1) // B * 16 + c
    ones_wide = jnp.ones((8, 16 * B), BF)
    ones_rows = jnp.ones((8, GROUP * B), BF)
    col_totals = jnp.zeros((8, 16 * B), F32)
    group = GROUP
    for a in range(0, 16, group):
        for i in range(group):
            chunk_copies[a + i].wait()
        keep = jnp.concatenate(
            [
                jnp.broadcast_to(
                    jnp.where(
                        (live[a + i : a + i + 1, :] > 0.5) & (col_block > r * 16 + a + i), 1.0, 0.0
                    ).astype(BF),
                    (B, 16 * B),
                )
                for i in range(group)
            ],
            axis=0,
        )
        rows = pl.ds(a * B, group * B)
        block = matrix[rows, :] * keep
        matrix[rows, :] = block
        col_totals = col_totals + jnp.dot(ones_rows, block, preferred_element_type=F32)
        totals = lax.dot_general(
            ones_wide, block, (((1,), (1,)), ((), ())), preferred_element_type=F32
        )
        for i in range(group):
            edsum[(a + i) % 2, (a + i) // 2 % 4, (a + i) // 8] = totals[:, i * B : (i + 1) * B]
        if a == 0:
            pl.semaphore_wait(barrier, NH * NL - 1 + NY - 1 + rest - 1)
            gram_cps = gram_start(0)
    for i in range(16):
        emsum[i // NL, i % NL] = col_totals[:, i * B : (i + 1) * B]
    diag_copy.wait()
    upper = lax.broadcasted_iota(jnp.int32, (B, B), 0) < lax.broadcasted_iota(jnp.int32, (B, B), 1)
    diag_value = jnp.where(upper, wdiag[...].astype(F32), 0.0).astype(BF)
    matrix[pl.ds(pl.multiple_of(c * B, B), B), pl.ds(pl.multiple_of(r * B, B), B)] = diag_value
    diag_degree = jnp.dot(ones_rows[:, :B], diag_value, preferred_element_type=F32) + lax.dot_general(
        ones_rows[:, :B], diag_value, (((1,), (1,)), ((), ())), preferred_element_type=F32
    )

    cps_c = rs_core(edsum, erc)
    cps_r = [
        send(emsum.at[(y + d) % NY], ery.at[d - 1], row_of((y + d) % NY, l), c)
        for d in range(1, NY)
    ]
    gram_cps = gram_z(0, gram_cps)
    wait_all(cps_c)
    ed1[...] = edsum[core] + erc[...]
    cps_c = [
        send(ed1.at[(x + d) % NX], erx.at[d - 1], *device_x((x + d) % NX)) for d in range(1, NX)
    ]
    flip(0)
    wait_all(cps_r)
    em1[...] = ((emsum[y] + ery[0]) + ery[1]) + ery[2]
    cps_r = rs_l(em1, erl)
    gram_cps = gram_y(0, gram_cps)
    flip(1)
    wait_all(cps_c)
    ed2[...] = ((ed1[x] + erx[0]) + erx[1]) + erx[2]
    cps_c = rs_h(ed2, erz)
    gram_cps = gram_all(0, gram_cps)
    wait_all(cps_r)
    wait_all(cps_c)
    degree = (ed2[h] + erz[...]) + (((em1[l] + erl[0]) + erl[1]) + erl[2]) + diag_degree
    inverse_root = jnp.broadcast_to(1.0 / jnp.sqrt(degree[0:1, :]), (K, B))
    factor = gram_end(0, gram_cps)
    panel = jnp.dot(factor, panel, precision=HI, preferred_element_type=F32)

    half = 8 * B
    wide = STEP * B

    for t in range(ITERS):
        vectors = (inverse_root * panel).astype(BF)
        vsend[t] = vectors
        vrow[t, c] = vectors
        vcol[t, r] = vectors
        own = vsend.at[t]
        cps_h = send(own, vrow.at[t, c], r, col_of(1 - h, e))
        cps_l = [
            send(own, vcol.at[t, r], row_of(y, (l + d) % NL), c) for d in range(1, NL)
        ]
        cps_y = [
            send(own, vcol.at[t, r], row_of((y + d) % NY, l), c) for d in range(1, NY)
        ]
        if t > 0:
            gram_local(t, panel)
            gram_cps = gram_start(t)
        cps_e = [
            send(own, vrow.at[t, c], r, col_of(h, (e + d) % rest)) for d in range(1, rest)
        ]
        for d in range(1, NL):
            cps_l[d - 1].wait_recv()
            got = vcol.at[t, row_of(y, (l - d + NL) % NL)]
            for f in range(1, NY):
                cps_y.append(send(got, got, row_of((y + f) % NY, l), c))
        cps_h.wait_recv()
        got = vrow.at[t, col_of(1 - h, e)]
        cps_far = [send(got, got, r, col_of(h, (e + d) % rest)) for d in range(1, rest)]
        if t > 0:
            gram_cps = gram_z(t, gram_cps)

        wait_all(cps_e)
        near = jnp.concatenate([vrow[t, h * rest + i] for i in range(rest)], axis=1)

        def mirror_near(j, _):
            cols = pl.ds(pl.multiple_of(j * wide, wide), wide)
            out = jnp.dot(
                near,
                matrix[pl.ds(pl.multiple_of(h * half, half), half), cols],
                preferred_element_type=F32,
            )
            for i in range(STEP):
                msum[t, j * (STEP // 4) + i // 4, i % 4] = out[:, i * B : (i + 1) * B]
            return 0

        lax.fori_loop(0, 16 // STEP, mirror_near, 0)
        wait_all(cps_y[: NY - 1])
        around = [(y + d) % NY for d in range(1, NY)]
        early = jnp.concatenate(
            [vcol[t, y * NL + i] for i in range(NL)] + [vcol[t, row_of(yy, l)] for yy in around],
            axis=1,
        )

        def stored_rows(blocks, cols):
            return jnp.concatenate(
                [flipped[pl.ds(pl.multiple_of(i * B, B), B), cols] for i in blocks], axis=0
            )

        def direct_near(j, _):
            cols = pl.ds(pl.multiple_of(j * wide, wide), wide)
            out = jnp.dot(
                early,
                stored_rows([y * NL + i for i in range(NL)] + [row_of(yy, l) for yy in around], cols),
                preferred_element_type=F32,
            )
            for i in range(STEP):
                b = j * STEP + i
                dsum[t, i % 2, b // 2 % 4, b // 8] = out[:, i * B : (i + 1) * B]
            return 0

        lax.fori_loop(0, 16 // STEP, direct_near, 0)
        def forwarded(d):
            return [row_of(yy, (l + NL - d) % NL) for yy in around]

        wait_all(cps_y[NY - 1 : 2 * (NY - 1)])
        middle = jnp.concatenate([vcol[t, i] for i in forwarded(1)], axis=1)

        def direct_middle(j, _):
            cols = pl.ds(pl.multiple_of(j * wide, wide), wide)
            out = jnp.dot(middle, stored_rows(forwarded(1), cols), preferred_element_type=F32)
            for i in range(STEP):
                b = j * STEP + i
                dsum[t, i % 2, b // 2 % 4, b // 8] += out[:, i * B : (i + 1) * B]
            return 0

        lax.fori_loop(0, 16 // STEP, direct_middle, 0)
        wait_all(cps_y[2 * (NY - 1) :])
        late = forwarded(2) + forwarded(3)
        others = jnp.concatenate([vcol[t, i] for i in late], axis=1)

        def direct_far(parity):
            stored = jnp.concatenate(
                [
                    stored_rows(late, pl.ds(pl.multiple_of((2 * i + parity) * B, B), B))
                    for i in range(8)
                ],
                axis=1,
            )
            out = jnp.dot(others, stored, preferred_element_type=F32)
            for i in range(8):
                dsum[t, parity, i % 4, i // 4] += out[:, i * B : (i + 1) * B]

        direct_far(1 - core)
        cps_c = rs_core(dsum.at[t], rc.at[t])
        if t > 0:
            gram_cps = gram_y(t, gram_cps)
        wait_all(cps_far)
        far = jnp.concatenate([vrow[t, (1 - h) * rest + i] for i in range(rest)], axis=1)

        def mirror_far(j, _):
            cols = pl.ds(pl.multiple_of(j * wide, wide), wide)
            out = jnp.dot(
                far,
                matrix[pl.ds(pl.multiple_of((1 - h) * half, half), half), cols],
                preferred_element_type=F32,
            )
            for i in range(STEP):
                msum[t, j * (STEP // 4) + i // 4, i % 4] += out[:, i * B : (i + 1) * B]
            return 0

        lax.fori_loop(0, 16 // STEP, mirror_far, 0)
        cps_r = ring_start(msum.at[t], ym.at[t], yq.at[t], y, device_y)
        direct_far(core)
        wait_all(cps_c)
        d1[t] = dsum[t, core] + rc[t]
        cps_c = ring_start(d1.at[t], xm.at[t], xq.at[t], x, device_x)
        if t > 0:
            gram_cps = gram_all(t, gram_cps)
        ring_end(cps_c, d1.at[t], xq.at[t], x, d2.at[t])
        d3[t] = d2[t, 1 - h].astype(BF)
        cps_c = [send(d3.at[t], rz.at[t], r, col_of(1 - h, e))]
        ring_end(cps_r, msum.at[t], yq.at[t], y, m1.at[t])
        m2[t] = m1[t].astype(BF)
        cps_r = rs_l(m2.at[t], rl.at[t])
        if t > 0:
            factor = gram_end(t, gram_cps)
        wait_all(cps_r)
        wait_all(cps_c)
        product = (d2[t, h] + rz[t].astype(F32)) + (
            ((m1[t, l] + rl[t, 0].astype(F32)) + rl[t, 1].astype(F32)) + rl[t, 2].astype(F32)
        )
        panel = panel + inverse_root * product
        if t > 0:
            panel = jnp.dot(factor, panel, precision=HI, preferred_element_type=F32)

    gram_local(ITERS, panel)
    gram_cps = gram_start(ITERS)
    done = len(pending)
    for cp in pending[: done - 7]:
        cp.wait_send()
    del pending[: done - 7]
    gram_cps = gram_z(ITERS, gram_cps)
    gram_cps = gram_y(ITERS, gram_cps)
    gram_cps = gram_all(ITERS, gram_cps)
    factor = gram_end(ITERS, gram_cps)
    out_ref[...] = jnp.dot(factor, panel, precision=HI, preferred_element_type=F32)
    for cp in pending:
        cp.wait_send()


def copies():
    gram = 7 + 3 + 7 + 7
    degrees = 1 + 3 + 1 + 3 + 3
    scatter = 1 + 3 + 1 + 3 + 3
    gather = 1 + 3 + 7 + 3 + 9 + 7
    return (ITERS + 1) * gram + degrees + ITERS * (scatter + gather)


def local(start_vectors, cluster_order, weights, block_mask):
    vm = pltpu.VMEM
    n = ITERS
    blk = (K, B)
    eblk = (8, B)
    scratch = [
        vm(blk, F32),
        vm((1, B), jnp.int32),
        vm((16, 1, 16), jnp.int32),
        vm((16 * B, 16 * B), BF),
        vm((16 * B, 16 * B), BF),
        vm((B, B), BF),
        vm((n,) + blk, BF),
        vm((n, 16) + blk, BF),
        vm((n, 16) + blk, BF),
        vm((n, NC, NX, NH) + blk, F32),
        vm((n, NX, NH) + blk, F32),
        vm((n, NH) + blk, F32),
        vm((n,) + blk, BF),
        vm((n, NX, NH) + blk, F32),
        vm((n, NX - 1, NH) + blk, BF),
        vm((n, NX, NH) + blk, BF),
        vm((n,) + blk, BF),
        vm((n, NY, NL) + blk, F32),
        vm((n, NL) + blk, F32),
        vm((n, NL) + blk, BF),
        vm((n, NY - 1, NL) + blk, BF),
        vm((n, NY, NL) + blk, BF),
        vm((n, NL - 1) + blk, BF),
        vm((NC, NX, NH) + eblk, F32),
        vm((NX, NH) + eblk, F32),
        vm((NH,) + eblk, F32),
        vm((NX, NH) + eblk, F32),
        vm((NX - 1, NH) + eblk, F32),
        vm(eblk, F32),
        vm((NY, NL) + eblk, F32),
        vm((NL,) + eblk, F32),
        vm((NY - 1, NL) + eblk, F32),
        vm((NL - 1,) + eblk, F32),
        vm((n + 1, 8) + eblk, F32),
        vm((n + 1, 7) + eblk, F32),
        vm((n + 1,) + eblk, F32),
        vm((n + 1, 3) + eblk, F32),
        vm((n + 1,) + eblk, F32),
        vm((n + 1, 7) + eblk, F32),
        vm((n + 1, 8) + eblk, F32),
        pltpu.SemaphoreType.DMA((20,)),
        pltpu.SemaphoreType.DMA((copies(),)),
        pltpu.SemaphoreType.DMA((copies(),)),
    ]
    hbm = pl.BlockSpec(memory_space=pltpu.HBM)
    panel = pl.pallas_call(
        kernel,
        out_shape=jax.ShapeDtypeStruct(blk, F32),
        in_specs=[hbm] * 4,
        out_specs=pl.BlockSpec(memory_space=pltpu.VMEM),
        scratch_shapes=scratch,
        compiler_params=pltpu.CompilerParams(
            collective_id=0, has_side_effects=True, vmem_limit_bytes=50 * 1000 * 1000
        ),
    )(
        *[
            pltpu.with_memory_space_constraint(v, pltpu.HBM)
            for v in (start_vectors, cluster_order, block_mask, weights[:, 0, :])
        ]
    )
    return math.sqrt(16 * 16 * B) * panel


def solution(mesh):
    placed = (
        P(None, ("row", "col")),
        P(("row", "col"), None),
        P("row", "col", None),
        P("row", "col", None),
    )
    return jax.shard_map(
        local, mesh=mesh, in_specs=placed, out_specs=P(None, ("row", "col")), check_vma=False
    )
```

```python
import functools
import math

import jax
import jax.numpy as jnp
from jax import lax
from jax.experimental import pallas as pl
from jax.experimental.pallas import tpu as pltpu
from jax.sharding import PartitionSpec as P

ITERS = 3
K = 64
B = 128
GROUP = 4
STEP = 8
FLIP = 256
NY, NL, NH, NX, NC = 4, 4, 2, 4, 2
MESH = pl.DeviceIdType.MESH
HI = lax.Precision.HIGHEST
F32 = jnp.float32
BF = jnp.bfloat16


def inverse_factor(blocks):
    groups = K // 8
    lane = lax.broadcasted_iota(jnp.int32, (8, 2 * K), 1)
    sub = lax.broadcasted_iota(jnp.int32, (8, 2 * K), 0)
    rows = [
        jnp.where(lane < K, (lane == sub + 8 * g).astype(F32), blocks[g]) for g in range(groups)
    ]

    def row_of_all(value, k):
        return jnp.broadcast_to(value[k : k + 1, :], (8, 2 * K))

    def column_of_all(value, j):
        return jnp.broadcast_to(value[:, K + j : K + j + 1], (8, 2 * K))

    out = []
    for b in range(groups):
        block = rows[b]
        columns = [column_of_all(block, 8 * b + m) for m in range(8)]
        pivots = {(k, m): row_of_all(columns[m], k) for m in range(8) for k in range(m, 8)}
        lower, inverses, reduced = {}, [], []
        for m in range(0, 8, 2):
            n = m + 1
            first, cross, second = pivots[m, m], pivots[n, m], pivots[n, n]
            one = 1.0 / first
            two = first * (1.0 / (first * second - cross * cross))
            inverses += [one, two]
            lower[n, m] = cross * one
            pivots[n, n] = second - cross * lower[n, m]
            for k in range(m + 2, 8):
                lower[k, m] = pivots[k, m] * one
                pivots[k, n] = pivots[k, n] - pivots[k, m] * lower[n, m]
                lower[k, n] = pivots[k, n] * two
            for k in range(m + 2, 8):
                for i in range(m + 2, k + 1):
                    pivots[k, i] = (pivots[k, i] - lower[k, m] * pivots[i, m]) - lower[
                        k, n
                    ] * pivots[i, n]
        for k in range(8):
            value = row_of_all(block, k)
            for m in range(k):
                value = value - lower[k, m] * reduced[m]
            reduced.append(value)
        if b + 1 < groups:
            solved = [None] * 8
            for k in reversed(range(8)):
                value = reduced[k] * inverses[k]
                for n in range(k + 1, 8):
                    value = value - lower[n, k] * solved[n]
                solved[k] = value
            for g in range(b + 1, groups):
                value = rows[g]
                for k in range(8):
                    value = value - column_of_all(rows[g], 8 * b + k) * solved[k]
                rows[g] = value
        result = jnp.zeros((8, 2 * K), F32)
        for k in range(8):
            result = jnp.where(sub == k, reduced[k] * (1.0 / jnp.sqrt(pivots[k, k])), result)
        out.append(result)
    return jnp.concatenate(out, axis=0)[:, :K]


def kernel(
    start_hbm,
    order_hbm,
    mask_hbm,
    w_ref,
    out_ref,
    start_ref,
    order_ref,
    mask_ref,
    matrix,
    flipped,
    wdiag,
    vsend,
    vrow,
    vcol,
    dsum,
    d1,
    d2,
    d3,
    rc,
    xq,
    xm,
    rz,
    msum,
    m1,
    m2,
    yq,
    ym,
    rl,
    edsum,
    ed1,
    ed2,
    erc,
    erx,
    erz,
    emsum,
    em1,
    ery,
    erl,
    gs,
    ga,
    g1,
    g2,
    gz,
    gf,
    wsem,
    ssem,
    rsem,
):
    r = lax.axis_index("row")
    c = lax.axis_index("col")
    y, l = r // NL, r % NL
    h, e = c // (NX * NC), c % (NX * NC)
    x, core = e // NC, e % NC
    z = h * NL + l
    rest = NX * NC

    def col_of(hh, ee):
        return hh * rest + ee

    def row_of(yy, ll):
        return yy * NL + ll

    def device_ye(d):
        return row_of((y + d // rest) % NY, l), col_of(h, (e + d) % rest)

    barrier = pltpu.get_barrier_semaphore()
    for d in range(1, NH * NL):
        zz = (z + d) % (NH * NL)
        pl.semaphore_signal(
            barrier,
            inc=1,
            device_id=(row_of(y, zz % NL), col_of(zz // NL, e)),
            device_id_type=MESH,
        )
    for d in range(1, NY * rest):
        pl.semaphore_signal(
            barrier, inc=1, device_id=device_ye(d), device_id_type=MESH
        )

    local_copies = []
    for i, (src, dst) in enumerate(
        ((order_hbm, order_ref), (start_hbm, start_ref), (mask_hbm, mask_ref))
    ):
        cp = pltpu.make_async_copy(src, dst, wsem.at[17 + i])
        cp.start()
        local_copies.append(cp)
    chunk_copies = []
    for a in range(16):
        cp = pltpu.make_async_copy(
            w_ref.at[pl.ds(a * B, B), :], matrix.at[pl.ds(a * B, B), :], wsem.at[a]
        )
        cp.start()
        chunk_copies.append(cp)
    diag_copy = pltpu.make_async_copy(
        w_ref.at[pl.ds(pl.multiple_of(c * B, B), B), pl.ds(pl.multiple_of(r * B, B), B)],
        wdiag,
        wsem.at[16],
    )
    diag_copy.start()

    count = [0]
    pending = []

    def send(src, dst, row, col):
        index = count[0]
        count[0] += 1
        cp = pltpu.make_async_remote_copy(
            src_ref=src,
            dst_ref=dst,
            send_sem=ssem.at[index],
            recv_sem=rsem.at[index],
            device_id=(row, col),
            device_id_type=MESH,
        )
        cp.start()
        pending.append(cp)
        return cp

    def wait_all(cps):
        for cp in cps:
            cp.wait_recv()

    def gram_local(t, panel):
        gram = lax.dot_general(
            panel, panel, (((1,), (1,)), ((), ())), precision=HI, preferred_element_type=F32
        )
        for g in range(8):
            gs[t, g] = jnp.concatenate(
                [gram[8 * g : 8 * g + 4], gram[8 * g + 4 : 8 * g + 8]], axis=1
            )

    def gram_start(t):
        return [
            send(gs.at[t, (e + d) % rest], ga.at[t, d - 1], r, col_of(h, (e + d) % rest))
            for d in range(1, rest)
        ]

    def gram_z(t, cps):
        wait_all(cps)
        total = gs[t, e]
        for d in range(rest - 1):
            total = total + ga[t, d]
        g1[t] = total
        out = []
        for d in range(1, NH * NL):
            zz = (z + d) % (NH * NL)
            out.append(send(g1.at[t], gz.at[t, d - 1], row_of(y, zz % NL), col_of(zz // NL, e)))
        return out

    def gram_all(t, cps):
        wait_all(cps)
        total = g1[t]
        for d in range(NH * NL - 1):
            total = total + gz[t, d]
        g2[t] = total
        gf[t, y, e] = total
        return [
            send(g2.at[t], gf.at[t, y, e], *device_ye(d)) for d in range(1, NY * rest)
        ]

    def gram_end(t, cps):
        wait_all(cps)
        blocks = []
        for g in range(8):
            half_block = (gf[t, 0, g] + gf[t, 1, g]) + (gf[t, 2, g] + gf[t, 3, g])
            blocks.append(
                jnp.concatenate([pltpu.roll(half_block, K, 1), half_block], axis=0)
            )
        return inverse_factor(blocks)

    def rs_core(src, dst):
        return [send(src.at[1 - core], dst, r, col_of(h, x * NC + 1 - core))]

    def rs_h(last, dst):
        return [send(last.at[1 - h], dst, r, col_of(1 - h, e))]

    def rs_l(mid, dst):
        out = []
        for d in range(1, NL):
            ll = (l + d) % NL
            out.append(send(mid.at[ll], dst.at[d - 1], row_of(y, ll), c))
        return out

    def ring_start(src, short, q, p, device):
        short[...] = src[...].astype(BF)
        return [
            send(short.at[(p + d) % 4], q.at[d - 1], *device((p + d) % 4)) for d in (2, 1, 3)
        ]

    def ring_end(cps, src, q, p, dst):
        wait_all(cps)
        dst[...] = (src[p] + q[0].astype(F32)) + (q[1].astype(F32) + q[2].astype(F32))

    def device_x(p):
        return r, col_of(h, p * NC + core)

    def device_y(p):
        return row_of(p, l), c

    def flip(part):
        def step(j, _):
            rows = pl.ds(pl.multiple_of(j * FLIP, FLIP), FLIP)
            flipped[:, rows] = matrix[rows, :].T
            return 0

        count = 16 * B // FLIP // 2
        lax.fori_loop(part * count, (part + 1) * count, step, 0)

    local_copies[0].wait()
    local_copies[1].wait()
    pick = (
        lax.broadcasted_iota(jnp.int32, (B, B), 0) == jnp.broadcast_to(order_ref[...], (B, B))
    ).astype(F32)
    panel = jnp.dot(start_ref[...], pick, precision=HI, preferred_element_type=F32)
    gram_local(0, panel)

    local_copies[2].wait()
    mask = jnp.concatenate([mask_ref[a] for a in range(16)], axis=0)
    spread = (
        lax.broadcasted_iota(jnp.int32, (16, 16 * B), 1) // B
        == lax.broadcasted_iota(jnp.int32, (16, 16 * B), 0)
    ).astype(F32)
    live = jnp.dot((mask > 0).astype(F32), spread, preferred_element_type=F32)
    col_block = lax.broadcasted_iota(jnp.int32, (1, 16 * B), 1) // B * 16 + c
    ones_wide = jnp.ones((8, 16 * B), BF)
    ones_rows = jnp.ones((8, GROUP * B), BF)
    col_totals = jnp.zeros((8, 16 * B), F32)
    group = GROUP
    for a in range(0, 16, group):
        for i in range(group):
            chunk_copies[a + i].wait()
        keep = jnp.concatenate(
            [
                jnp.broadcast_to(
                    jnp.where(
                        (live[a + i : a + i + 1, :] > 0.5) & (col_block > r * 16 + a + i), 1.0, 0.0
                    ).astype(BF),
                    (B, 16 * B),
                )
                for i in range(group)
            ],
            axis=0,
        )
        rows = pl.ds(a * B, group * B)
        block = matrix[rows, :] * keep
        matrix[rows, :] = block
        col_totals = col_totals + jnp.dot(ones_rows, block, preferred_element_type=F32)
        totals = lax.dot_general(
            ones_wide, block, (((1,), (1,)), ((), ())), preferred_element_type=F32
        )
        for i in range(group):
            edsum[(a + i) % 2, (a + i) // 2 % 4, (a + i) // 8] = totals[:, i * B : (i + 1) * B]
        if a == 0:
            pl.semaphore_wait(barrier, NH * NL - 1 + NY * rest - 1)
            gram_cps = gram_start(0)
    for i in range(16):
        emsum[i // NL, i % NL] = col_totals[:, i * B : (i + 1) * B]
    diag_copy.wait()
    upper = lax.broadcasted_iota(jnp.int32, (B, B), 0) < lax.broadcasted_iota(jnp.int32, (B, B), 1)
    diag_value = jnp.where(upper, wdiag[...].astype(F32), 0.0).astype(BF)
    matrix[pl.ds(pl.multiple_of(c * B, B), B), pl.ds(pl.multiple_of(r * B, B), B)] = diag_value
    diag_degree = jnp.dot(ones_rows[:, :B], diag_value, preferred_element_type=F32) + lax.dot_general(
        ones_rows[:, :B], diag_value, (((1,), (1,)), ((), ())), preferred_element_type=F32
    )

    cps_c = rs_core(edsum, erc)
    cps_r = [
        send(emsum.at[(y + d) % NY], ery.at[d - 1], row_of((y + d) % NY, l), c)
        for d in range(1, NY)
    ]
    gram_cps = gram_z(0, gram_cps)
    wait_all(cps_c)
    ed1[...] = edsum[core] + erc[...]
    cps_c = [
        send(ed1.at[(x + d) % NX], erx.at[d - 1], *device_x((x + d) % NX)) for d in range(1, NX)
    ]
    flip(0)
    wait_all(cps_r)
    em1[...] = ((emsum[y] + ery[0]) + ery[1]) + ery[2]
    cps_r = rs_l(em1, erl)
    gram_cps = gram_all(0, gram_cps)
    flip(1)
    wait_all(cps_c)
    ed2[...] = ((ed1[x] + erx[0]) + erx[1]) + erx[2]
    cps_c = rs_h(ed2, erz)
    wait_all(cps_r)
    wait_all(cps_c)
    degree = (ed2[h] + erz[...]) + (((em1[l] + erl[0]) + erl[1]) + erl[2]) + diag_degree
    inverse_root = jnp.broadcast_to(1.0 / jnp.sqrt(degree[0:1, :]), (K, B))
    factor = gram_end(0, gram_cps)
    panel = jnp.dot(factor, panel, precision=HI, preferred_element_type=F32)

    half = 8 * B
    wide = STEP * B

    for t in range(ITERS):
        vectors = (inverse_root * panel).astype(BF)
        vsend[t] = vectors
        vrow[t, c] = vectors
        vcol[t, r] = vectors
        own = vsend.at[t]
        cps_h = send(own, vrow.at[t, c], r, col_of(1 - h, e))
        cps_l = [
            send(own, vcol.at[t, r], row_of(y, (l + d) % NL), c) for d in range(1, NL)
        ]
        cps_y = [
            send(own, vcol.at[t, r], row_of((y + d) % NY, l), c) for d in range(1, NY)
        ]
        if t > 0:
            gram_local(t, panel)
            gram_cps = gram_start(t)
        cps_e = [
            send(own, vrow.at[t, c], r, col_of(h, (e + d) % rest)) for d in range(1, rest)
        ]
        for d in range(1, NL):
            cps_l[d - 1].wait_recv()
            got = vcol.at[t, row_of(y, (l - d + NL) % NL)]
            for f in range(1, NY):
                cps_y.append(send(got, got, row_of((y + f) % NY, l), c))
        cps_h.wait_recv()
        got = vrow.at[t, col_of(1 - h, e)]
        cps_far = [send(got, got, r, col_of(h, (e + d) % rest)) for d in range(1, rest)]
        if t > 0:
            gram_cps = gram_z(t, gram_cps)

        wait_all(cps_e)
        near = jnp.concatenate([vrow[t, h * rest + i] for i in range(rest)], axis=1)

        def mirror_near(j, _):
            cols = pl.ds(pl.multiple_of(j * wide, wide), wide)
            out = jnp.dot(
                near,
                matrix[pl.ds(pl.multiple_of(h * half, half), half), cols],
                preferred_element_type=F32,
            )
            for i in range(STEP):
                msum[t, j * (STEP // 4) + i // 4, i % 4] = out[:, i * B : (i + 1) * B]
            return 0

        lax.fori_loop(0, 16 // STEP, mirror_near, 0)
        wait_all(cps_y[: NY - 1])
        around = [(y + d) % NY for d in range(1, NY)]
        early = jnp.concatenate(
            [vcol[t, y * NL + i] for i in range(NL)] + [vcol[t, row_of(yy, l)] for yy in around],
            axis=1,
        )

        def stored_rows(blocks, cols):
            return jnp.concatenate(
                [flipped[pl.ds(pl.multiple_of(i * B, B), B), cols] for i in blocks], axis=0
            )

        def direct_near(j, _):
            cols = pl.ds(pl.multiple_of(j * wide, wide), wide)
            out = jnp.dot(
                early,
                stored_rows([y * NL + i for i in range(NL)] + [row_of(yy, l) for yy in around], cols),
                preferred_element_type=F32,
            )
            for i in range(STEP):
                b = j * STEP + i
                dsum[t, i % 2, b // 2 % 4, b // 8] = out[:, i * B : (i + 1) * B]
            return 0

        lax.fori_loop(0, 16 // STEP, direct_near, 0)
        def forwarded(d):
            return [row_of(yy, (l + NL - d) % NL) for yy in around]

        wait_all(cps_y[NY - 1 : 2 * (NY - 1)])
        middle = jnp.concatenate([vcol[t, i] for i in forwarded(1)], axis=1)

        def direct_middle(j, _):
            cols = pl.ds(pl.multiple_of(j * wide, wide), wide)
            out = jnp.dot(middle, stored_rows(forwarded(1), cols), preferred_element_type=F32)
            for i in range(STEP):
                b = j * STEP + i
                dsum[t, i % 2, b // 2 % 4, b // 8] += out[:, i * B : (i + 1) * B]
            return 0

        lax.fori_loop(0, 16 // STEP, direct_middle, 0)
        wait_all(cps_y[2 * (NY - 1) :])
        late = forwarded(2) + forwarded(3)
        others = jnp.concatenate([vcol[t, i] for i in late], axis=1)

        def direct_far(parity):
            stored = jnp.concatenate(
                [
                    stored_rows(late, pl.ds(pl.multiple_of((2 * i + parity) * B, B), B))
                    for i in range(8)
                ],
                axis=1,
            )
            out = jnp.dot(others, stored, preferred_element_type=F32)
            for i in range(8):
                dsum[t, parity, i % 4, i // 4] += out[:, i * B : (i + 1) * B]

        direct_far(1 - core)
        cps_c = rs_core(dsum.at[t], rc.at[t])
        wait_all(cps_far)
        far = jnp.concatenate([vrow[t, (1 - h) * rest + i] for i in range(rest)], axis=1)

        def mirror_far(j, _):
            cols = pl.ds(pl.multiple_of(j * wide, wide), wide)
            out = jnp.dot(
                far,
                matrix[pl.ds(pl.multiple_of((1 - h) * half, half), half), cols],
                preferred_element_type=F32,
            )
            for i in range(STEP):
                msum[t, j * (STEP // 4) + i // 4, i % 4] += out[:, i * B : (i + 1) * B]
            return 0

        lax.fori_loop(0, 16 // STEP, mirror_far, 0)
        cps_r = ring_start(msum.at[t], ym.at[t], yq.at[t], y, device_y)
        direct_far(core)
        wait_all(cps_c)
        d1[t] = dsum[t, core] + rc[t]
        cps_c = ring_start(d1.at[t], xm.at[t], xq.at[t], x, device_x)
        if t > 0:
            gram_cps = gram_all(t, gram_cps)
        ring_end(cps_c, d1.at[t], xq.at[t], x, d2.at[t])
        d3[t] = d2[t, 1 - h].astype(BF)
        cps_c = [send(d3.at[t], rz.at[t], r, col_of(1 - h, e))]
        ring_end(cps_r, msum.at[t], yq.at[t], y, m1.at[t])
        m2[t] = m1[t].astype(BF)
        cps_r = rs_l(m2.at[t], rl.at[t])
        if t > 0:
            factor = gram_end(t, gram_cps)
        wait_all(cps_r)
        wait_all(cps_c)
        product = (d2[t, h] + rz[t].astype(F32)) + (
            ((m1[t, l] + rl[t, 0].astype(F32)) + rl[t, 1].astype(F32)) + rl[t, 2].astype(F32)
        )
        panel = panel + inverse_root * product
        if t > 0:
            panel = jnp.dot(factor, panel, precision=HI, preferred_element_type=F32)

    gram_local(ITERS, panel)
    gram_cps = gram_start(ITERS)
    done = len(pending)
    for cp in pending[: done - 7]:
        cp.wait_send()
    del pending[: done - 7]
    gram_cps = gram_z(ITERS, gram_cps)
    gram_cps = gram_all(ITERS, gram_cps)
    factor = gram_end(ITERS, gram_cps)
    out_ref[...] = jnp.dot(factor, panel, precision=HI, preferred_element_type=F32)
    for cp in pending:
        cp.wait_send()


def copies():
    gram = 7 + 7 + 31
    degrees = 1 + 3 + 1 + 3 + 3
    scatter = 1 + 3 + 1 + 3 + 3
    gather = 1 + 3 + 7 + 3 + 9 + 7
    return (ITERS + 1) * gram + degrees + ITERS * (scatter + gather)


def local(start_vectors, cluster_order, weights, block_mask):
    vm = pltpu.VMEM
    n = ITERS
    blk = (K, B)
    eblk = (8, B)
    gblk = (4, B)
    scratch = [
        vm(blk, F32),
        vm((1, B), jnp.int32),
        vm((16, 1, 16), jnp.int32),
        vm((16 * B, 16 * B), BF),
        vm((16 * B, 16 * B), BF),
        vm((B, B), BF),
        vm((n,) + blk, BF),
        vm((n, 16) + blk, BF),
        vm((n, 16) + blk, BF),
        vm((n, NC, NX, NH) + blk, F32),
        vm((n, NX, NH) + blk, F32),
        vm((n, NH) + blk, F32),
        vm((n,) + blk, BF),
        vm((n, NX, NH) + blk, F32),
        vm((n, NX - 1, NH) + blk, BF),
        vm((n, NX, NH) + blk, BF),
        vm((n,) + blk, BF),
        vm((n, NY, NL) + blk, F32),
        vm((n, NL) + blk, F32),
        vm((n, NL) + blk, BF),
        vm((n, NY - 1, NL) + blk, BF),
        vm((n, NY, NL) + blk, BF),
        vm((n, NL - 1) + blk, BF),
        vm((NC, NX, NH) + eblk, F32),
        vm((NX, NH) + eblk, F32),
        vm((NH,) + eblk, F32),
        vm((NX, NH) + eblk, F32),
        vm((NX - 1, NH) + eblk, F32),
        vm(eblk, F32),
        vm((NY, NL) + eblk, F32),
        vm((NL,) + eblk, F32),
        vm((NY - 1, NL) + eblk, F32),
        vm((NL - 1,) + eblk, F32),
        vm((n + 1, 8) + gblk, F32),
        vm((n + 1, 7) + gblk, F32),
        vm((n + 1,) + gblk, F32),
        vm((n + 1,) + gblk, F32),
        vm((n + 1, 7) + gblk, F32),
        vm((n + 1, NY, 8) + gblk, F32),
        pltpu.SemaphoreType.DMA((20,)),
        pltpu.SemaphoreType.DMA((copies(),)),
        pltpu.SemaphoreType.DMA((copies(),)),
    ]
    hbm = pl.BlockSpec(memory_space=pltpu.HBM)
    panel = pl.pallas_call(
        kernel,
        out_shape=jax.ShapeDtypeStruct(blk, F32),
        in_specs=[hbm] * 4,
        out_specs=pl.BlockSpec(memory_space=pltpu.VMEM),
        scratch_shapes=scratch,
        compiler_params=pltpu.CompilerParams(
            collective_id=0, has_side_effects=True, vmem_limit_bytes=50 * 1000 * 1000
        ),
    )(
        *[
            pltpu.with_memory_space_constraint(v, pltpu.HBM)
            for v in (start_vectors, cluster_order, block_mask, weights[:, 0, :])
        ]
    )
    return math.sqrt(16 * 16 * B) * panel


def solution(mesh):
    placed = (
        P(None, ("row", "col")),
        P(("row", "col"), None),
        P("row", "col", None),
        P("row", "col", None),
    )
    return jax.shard_map(
        local, mesh=mesh, in_specs=placed, out_specs=P(None, ("row", "col")), check_vma=False
    )
```
